32 devices in a mesh: dp: 4 (over z), fsdp: 2 (over x), tensor: 4 (over y, core).
Axes of the slice: x: 2, y: 2, z: 4, core: 2. Of those that a mesh axis runs over, the one named last changes fastest.
Arguments:
- tokens: bfloat16 [32, 256, 768], P(('dp', 'fsdp')), may hold values from -6 to 6
- keep_mask: int32 [32, 256], P(('dp', 'fsdp')), may hold values 0 or 1
- crop_len: int32 [32], P(('dp', 'fsdp')), may hold values from 128 to 256
- pos_index: int32 [32], replicated, may hold values from 0 to 31, each once
- pos_keys: bfloat16 [32, 768], P(('dp', 'fsdp')), may hold values from -0.08984375 to 0.08984375
- key_queue: bfloat16 [16384, 768], P(('dp', 'fsdp')), may hold values from -0.08984375 to 0.08984375
- query_weight: bfloat16 [768, 768], P(None, 'tensor'), may hold values from -0.21875 to 0.21875
- query_bias: float32 [768], P('tensor'), may hold values from -1.25 to 1.25
- key_weight: bfloat16 [768, 768], P(None, 'tensor'), may hold values from -0.21875 to 0.21875
- value_weight: bfloat16 [768, 768], P(None, 'tensor'), may hold values from -0.21875 to 0.21875
- value_bias: float32 [768], P('tensor'), may hold values from -1.25 to 1.25
- out_weight: bfloat16 [768, 768], P('tensor'), may hold values from -0.875 to 0.875
- out_bias: float32 [768], replicated, may hold values from -1.25 to 1.25
- norm_gain: float32 [768], replicated, may hold values from 0.5 to 1.5
- norm_shift: float32 [768], replicated, may hold values from -1.25 to 1.25
- up_weight: bfloat16 [768, 3072], P(None, 'tensor'), may hold values from -0.21875 to 0.21875
- up_bias: float32 [3072], P('tensor'), may hold values from -1.25 to 1.25
- down_weight: bfloat16 [3072, 768], P('tensor'), may hold values from -0.109375 to 0.109375
- down_bias: float32 [768], replicated, may hold values from -1.25 to 1.25
- final_gain: float32 [768], replicated, may hold values from 0.5 to 1.5
- final_shift: float32 [768], replicated, may hold values from -0.625 to 0.625
Outputs:
- output: bfloat16 [32, 256, 768], P(('dp', 'fsdp', 'tensor'))
- input_grad: bfloat16 [32, 256, 768], P(('dp', 'fsdp', 'tensor'))
- query_weight_grad: float32 [768, 768], P(None, 'tensor')
- query_bias_grad: float32 [768], P('tensor')
- key_weight_grad: float32 [768, 768], P(None, 'tensor')
- value_weight_grad: float32 [768, 768], P(None, 'tensor')
- value_bias_grad: float32 [768], P('tensor')
- out_weight_grad: float32 [768, 768], P('tensor')
- out_bias_grad: float32 [768], replicated
- norm_gain_grad: float32 [768], replicated
- norm_shift_grad: float32 [768], replicated
- up_weight_grad: float32 [768, 3072], P(None, 'tensor')
- up_bias_grad: float32 [3072], P('tensor')
- down_weight_grad: float32 [3072, 768], P('tensor')
- down_bias_grad: float32 [768], replicated
- final_gain_grad: float32 [768], replicated
- final_shift_grad: float32 [768], replicated
- loss: float32 [], replicated
The draws below stay inside these ranges and needn't reach their ends.
Inputs may be any that keep to these rules, and one draw needn't show every extreme that they name: pos_index is a permutation of the crops.
All inputs are finite; a program needn't handle non-finite values. No bound on the sum of `keep_mask` on one device may be relied on, other than what follows from the above.
Results may differ from the reference program's by a relative error of at most 0.028.
Values may be sent and summed in bfloat16 or wider, within the bound.
No kernel may reach another device: no remote copies, remote signals or barrier semaphores. Data moves between devices by JAX's collectives and lax.ppermute only.
A program may use at most 128 MiB of HBM per device.

```python
import math
import jax
import jax.numpy as jnp
from jax import lax

D = 768
HEADS = 12
HEAD = 64
FF = 3072
LEN = 256
SEQS = 32
QUEUE = 16384


def place_ends(array, own_key, low, largest):
    dims = array.shape
    place = [jax.random.randint(jax.random.fold_in(own_key, axis), (), 0, dims[axis]) for axis in range(len(dims))]
    array = array.at[tuple(place)].set(low)
    longest = dims.index(max(dims))
    place[longest] = (place[longest] + 1) % dims[longest]
    return array.at[tuple(place)].set(largest)


def levels(key, extent, pieces, smallest, high):
    level, own = 1.0, jax.random.fold_in(key, 6)
    for position, shards_of in pieces:
        heights = jnp.exp(jax.random.uniform(jax.random.fold_in(own, position), (shards_of,), jnp.float32, smallest / len(pieces), high / len(pieces)))
        level = level * jnp.repeat(heights, extent[position] // shards_of).reshape([-1 if axis == position else 1 for axis in range(len(extent))])
    return level


def gaussian(own_key, shape, spread, bound, cuts=(), kind=jnp.bfloat16):
    drawn = jax.random.normal(own_key, shape, jnp.float32) * spread
    if len(cuts) > 0:
        drawn = levels(own_key, shape, cuts, -0.22, 0.18) * drawn
    return jnp.clip(drawn, min=-bound, max=bound).astype(kind)


def setup_inputs(seed: int = 0) -> dict:
    key_of = jax.random.split(jax.random.key(seed), 22)
    return {
        "tokens": gaussian(key_of[0], (SEQS, LEN, D), 1.0, 6.0, ((0, 8),)),
        "keep_mask": place_ends((jax.random.randint(key_of[1], (SEQS, LEN), 0, 10) < 9).astype(jnp.int32), jax.random.fold_in(key_of[1], 1), 0, 1),
        "crop_len": place_ends(jax.random.randint(key_of[2], (SEQS,), LEN // 2, LEN + 1), jax.random.fold_in(key_of[2], 1), LEN // 2, LEN).astype(jnp.int32),
        "pos_index": jax.random.permutation(key_of[3], SEQS).astype(jnp.int32),
        "pos_keys": gaussian(key_of[4], (SEQS, D), 0.015, 0.08984375, ((0, 8),)),
        "key_queue": gaussian(key_of[5], (QUEUE, D), 0.015, 0.08984375, ((0, 8),)),
        "query_weight": gaussian(key_of[6], (D, D), D ** -0.5, 0.21875, ((1, 4),)),
        "query_bias": gaussian(key_of[7], (D,), 0.2, 1.25, ((0, 4),), jnp.float32),
        "key_weight": gaussian(key_of[8], (D, D), D ** -0.5, 0.21875, ((1, 4),)),
        "value_weight": gaussian(key_of[9], (D, D), D ** -0.5, 0.21875, ((1, 4),)),
        "value_bias": gaussian(key_of[10], (D,), 0.2, 1.25, ((0, 4),), jnp.float32),
        "out_weight": gaussian(key_of[11], (D, D), (D // 16) ** -0.5, 0.875, ((0, 4),)),
        "out_bias": gaussian(key_of[12], (D,), 0.2, 1.25, (), jnp.float32),
        "norm_gain": jnp.clip(1.0 + 0.1 * jax.random.normal(key_of[13], (D,), jnp.float32), 0.5, 1.5),
        "norm_shift": gaussian(key_of[14], (D,), 0.2, 1.25, (), jnp.float32),
        "up_weight": gaussian(key_of[15], (D, FF), D ** -0.5, 0.21875, ((1, 4),)),
        "up_bias": gaussian(key_of[16], (FF,), 0.2, 1.25, ((0, 4),), jnp.float32),
        "down_weight": gaussian(key_of[17], (FF, D), FF ** -0.5, 0.109375, ((0, 4),)),
        "down_bias": gaussian(key_of[18], (D,), 0.2, 1.25, (), jnp.float32),
        "final_gain": jnp.clip(1.0 + 0.1 * jax.random.normal(key_of[19], (D,), jnp.float32), 0.5, 1.5),
        "final_shift": gaussian(key_of[20], (D,), 0.1, 0.625, (), jnp.float32),
    }


@jax.custom_vjp
def low(v):
    return lax.optimization_barrier(v.astype(jnp.bfloat16)).astype(jnp.float32)

@jax.custom_vjp
def low_back(v):
    return v

def low_keep(v):
    return (low(v), None)

def low_pass(kept, grad):
    return (grad,)

def back_keep(v):
    return (v, None)

def back_low(kept, grad):
    return (low(grad),)
low.defvjp(low_keep, low_pass)
low_back.defvjp(back_keep, back_low)
highest_precision = lax.Precision.HIGHEST
eps = 1e-12
inv_temp = 20.0
loss_scale = 256.0

def layer_norm(resid, gain, shift):
    center = resid - lax.optimization_barrier(jnp.mean(resid, axis=-1, keepdims=True))
    rstd = lax.rsqrt(lax.optimization_barrier(jnp.mean(center * center, axis=-1, keepdims=True)) + eps)
    return center * rstd * gain + shift

def compact_table(keep_mask, crop_len):
    places = jnp.arange(LEN, dtype=jnp.int32)
    kept = ((keep_mask == 1) | (places == 0)[None, :]) & (places[None, :] < crop_len[:, None])
    rank = jnp.cumsum(kept.astype(jnp.int32), axis=1) - 1
    table = kept[:, None, :] & (rank[:, None, :] == places[None, :, None])
    count = lax.optimization_barrier(jnp.sum(kept.astype(jnp.int32), axis=1))
    return (table.astype(jnp.float32), count)

def project(token_rows, weight_matrix):
    return jnp.einsum('ixw,wk->ixk', token_rows, weight_matrix, precision=highest_precision)

def layer_block(weights, tokens, table, count):
    query_weight, query_bias, key_weight, value_weight, value_bias, out_weight, out_bias, norm_gain, norm_shift, up_weight, up_bias, down_weight, down_bias, final_gain, final_shift = weights
    batch = tokens.shape[0]
    places = jnp.arange(LEN, dtype=jnp.int32)
    live = places[None, :] < count[:, None]
    compact = jnp.einsum('sjp,spd->sjd', table, tokens, precision=highest_precision)
    query = low(low_back(project(compact, query_weight) + query_bias)).reshape(batch, LEN, HEADS, HEAD)
    keys = low(low_back(project(compact, key_weight))).reshape(batch, LEN, HEADS, HEAD)
    values = low(low_back(project(compact, value_weight) + value_bias)).reshape(batch, LEN, HEADS, HEAD)
    scores = jnp.einsum('bqhd,bkhd->bhqk', query, keys, precision=highest_precision) * (1.0 / math.sqrt(HEAD))
    scores = jnp.where(live[:, None, None, :], scores, -1e+30)
    probs = jax.nn.softmax(scores, axis=-1)
    context_rows = low(low_back(jnp.einsum('bhqk,bkhd->bqhd', low(probs), values, precision=highest_precision)))
    context_rows = context_rows.reshape(batch, LEN, D)
    attn_out = low_back(project(context_rows, out_weight) + out_bias)
    mid = layer_norm(compact + attn_out, norm_gain, norm_shift)
    pre = low_back(project(low(mid), up_weight) + up_bias)
    hidden_state = low(jax.nn.gelu(pre, approximate=False))
    ffn_out = low_back(project(hidden_state, down_weight) + down_bias)
    result = layer_norm(mid + ffn_out, final_gain, final_shift)
    pooled = lax.optimization_barrier(jnp.sum(result * live[:, :, None].astype(result.dtype), axis=1)) / count[:, None].astype(result.dtype)
    return (result, pooled)

def reference(tokens, keep_mask, crop_len, pos_index, pos_keys, key_queue, query_weight, query_bias, key_weight, value_weight, value_bias, out_weight, out_bias, norm_gain, norm_shift, up_weight, up_bias, down_weight, down_bias, final_gain, final_shift):
    params = tuple((arr.astype(jnp.float32) for arr in (query_weight, query_bias, key_weight, value_weight, value_bias, out_weight, out_bias, norm_gain, norm_shift, up_weight, up_bias, down_weight, down_bias, final_gain, final_shift)))
    group = math.gcd(SEQS, max(1, 4096 // LEN))
    blocks = SEQS // group
    key_rows = math.gcd(QUEUE, 4096)
    masks = keep_mask.reshape(blocks, group, LEN)
    lengths = crop_len.reshape(blocks, group)
    positive = pos_keys.astype(jnp.float32)[pos_index]
    queue_blocks = key_queue.reshape(QUEUE // key_rows, key_rows, D)

    def forward(inputs, weights):

        def run_block(item):
            table, count = compact_table(item[1], item[2])
            return layer_block(weights, item[0], table, count)
        result, pooled = lax.map(jax.checkpoint(run_block), (inputs.reshape(blocks, group, LEN, D), masks, lengths))
        result = result.reshape(SEQS, LEN, D)
        pooled = pooled.reshape(SEQS, D)
        query_vec = low(pooled)
        pos_logit = lax.optimization_barrier(jnp.sum(query_vec * positive, axis=-1)) * inv_temp

        def key_block(block):
            logit = low_back(jnp.dot(query_vec, block.astype(jnp.float32).T, precision=highest_precision)) * inv_temp
            return jax.nn.logsumexp(logit, axis=1)
        partial_lse = lax.map(jax.checkpoint(key_block), queue_blocks)
        lse = jax.nn.logsumexp(jnp.concatenate([partial_lse, pos_logit[None, :]], axis=0), axis=0)
        return (result, jnp.sum(lse - pos_logit))
    (result, total), pull = jax.vjp(forward, tokens.astype(jnp.float32), params)
    input_grad, gradient_list = pull((jnp.zeros_like(result), jnp.ones_like(total) * loss_scale))
    return (result.astype(jnp.bfloat16), input_grad.astype(jnp.bfloat16), gradient_list[0], gradient_list[1], gradient_list[2], gradient_list[3], gradient_list[4], gradient_list[5], gradient_list[6], gradient_list[7], gradient_list[8], gradient_list[9], gradient_list[10], gradient_list[11], gradient_list[12], gradient_list[13], gradient_list[14], total / SEQS)
```

```python
import math

import jax
import jax.numpy as jnp
from jax import lax
from jax.experimental import pallas as pl
from jax.experimental.pallas import tpu as pltpu
from jax.sharding import PartitionSpec as P

HEAD = 64
eps = 1e-12
inv_temp = 20.0
loss_scale = 256.0
low = jnp.bfloat16
full = jnp.float32
LANES = 128

RELATIVE = (0, 2, 1, 3)


def dot(a, b, dims=((1,), (0,))):
    return lax.dot_general(a, b, (dims, ((), ())), preferred_element_type=full)


def swap(array, axis, stride):
    size = lax.axis_size(axis)
    return lax.ppermute(array, axis, [(i, i ^ stride) for i in range(size)])


def strides(axis):
    size = lax.axis_size(axis)
    assert size & (size - 1) == 0
    return [1 << k for k in range(size.bit_length() - 1)]


def tensor_gather(block):
    pair = jnp.stack([block, swap(block, "tensor", 2)])
    return jnp.concatenate([pair, swap(pair, "tensor", 1)])


def tensor_sum(parts):
    other = swap(parts[2:], "tensor", 1)
    far = swap((parts[1].astype(full) + other[1].astype(full)).astype(low), "tensor", 2)
    return parts[0].astype(full) + other[0].astype(full) + far.astype(full)


def group_sum(grad):
    rows = grad.shape[0] // 2
    f = lax.axis_index("fsdp")
    kept = lax.dynamic_slice_in_dim(grad, f * rows, rows, 0)
    sent = lax.dynamic_slice_in_dim(grad, (1 - f) * rows, rows, 0)
    part = kept.astype(full) + swap(sent, "fsdp", 1).astype(full)
    if lax.axis_size("dp") == 4:
        z = lax.axis_index("dp")
        part = part + lax.ppermute(part.astype(low), "dp", [(0, 1), (3, 2)]).astype(full)
        part = part.astype(low)
        total = part.astype(full) + lax.ppermute(part, "dp", [(1, 2), (2, 1)]).astype(full)
        total = total.astype(low)
        outer = lax.ppermute(total, "dp", [(1, 0), (2, 3)])
        total = jnp.where((z == 0) | (z == 3), outer, total)
    else:
        total = lax.psum(part, "dp").astype(low)
    other = swap(total, "fsdp", 1)
    first = jnp.where(f == 0, total, other)
    second = jnp.where(f == 0, other, total)
    return jnp.concatenate([first, second])


def norm_parts(resid):
    center = resid - jnp.mean(resid, axis=-1, keepdims=True)
    rstd = lax.rsqrt(jnp.mean(center * center, axis=-1, keepdims=True) + eps)
    return (center * rstd, rstd)


def norm_backward(scaled, normed, rstd):
    inner = jnp.mean(scaled, axis=-1, keepdims=True)
    along = jnp.mean(scaled * normed, axis=-1, keepdims=True)
    return rstd * (scaled - inner - normed * along)


def gelu_parts(pre):
    cdf = 0.5 * (1.0 + lax.erf(pre * math.sqrt(0.5)))
    slope = cdf + pre * (jnp.exp(-0.5 * pre * pre) * (1.0 / math.sqrt(2.0 * math.pi)))
    return (pre * cdf, slope)


def attend_kernel(
    order, lens, mask, tokens, wq, wk, wv, wo, bq, bv, compact_out, q_out, k_out, v_out, p_out, ctx_out, part_out, table_out, count_out
):
    b = pl.program_id(0)
    length = mask.shape[-1]
    crop_len = lens[order[b]]
    lane = lax.broadcasted_iota(jnp.int32, (1, length), 1)
    kept = jnp.where(((mask[0] == 1) | (lane == 0)) & (lane < crop_len), 1.0, 0.0)
    rows = lax.broadcasted_iota(jnp.int32, (length, length), 0)
    cols = lax.broadcasted_iota(jnp.int32, (length, length), 1)
    upto = jnp.where(rows <= cols, 1.0, 0.0).astype(low)
    rank = dot(jnp.broadcast_to(kept, (8, length)).astype(low), upto)[0:1]
    place = jnp.where(kept > 0.0, rank - 1.0, -1.0)
    table = jnp.where(place == rows.astype(full), 1.0, 0.0).astype(low)
    count = jnp.sum(kept)

    @pl.when(b == 0)
    def _():
        table_out[...] = table
        count_out[...] = jnp.full(count_out.shape, count, full)

    compact = dot(table, tokens[0]).astype(low)
    compact_out[0] = compact
    query = (dot(compact, wq[...]) + bq[...]).astype(low)
    keys = dot(compact, wk[...]).astype(low)
    values = (dot(compact, wv[...]) + bv[...]).astype(low)
    q_out[0], k_out[0], v_out[0] = query, keys, values
    live = lane.astype(full) < count
    contexts = []
    for h in range(query.shape[1] // HEAD):
        span = slice(h * HEAD, (h + 1) * HEAD)
        scores = dot(query[:, span], keys[:, span], ((1,), (1,))) * (1.0 / math.sqrt(HEAD))
        scores = jnp.where(live, scores, -1e30)
        expo = jnp.exp(scores - jnp.max(scores, axis=1, keepdims=True))
        probs = (expo / jnp.sum(expo, axis=1, keepdims=True)).astype(low)
        p_out[0, h] = probs
        contexts.append(dot(probs, values[:, span]).astype(low))
    context = jnp.concatenate(contexts, axis=1)
    ctx_out[0] = context
    part_out[0] = dot(context, wo[...]).astype(low)


def attend(tokens, keep_mask, crop_len, order, wq, wk, wv, wo, bq, bv):
    seqs, length, width = tokens.shape
    mine = wq.shape[1]
    heads = mine // HEAD

    def const(shape):
        return pl.BlockSpec(shape, lambda b, *_: (0,) * len(shape))

    def per(*shape):
        return pl.BlockSpec((1, *shape), lambda b, *_: (b,) + (0,) * len(shape))

    def picked(*shape):
        return pl.BlockSpec((1, *shape), lambda b, order, lens: (order[b],) + (0,) * len(shape))

    S = jax.ShapeDtypeStruct
    return pl.pallas_call(
        attend_kernel,
        grid_spec=pltpu.PrefetchScalarGridSpec(
            num_scalar_prefetch=2,
            grid=(seqs,),
            in_specs=[
                picked(1, length),
                picked(length, width),
                const((width, mine)),
                const((width, mine)),
                const((width, mine)),
                const((mine, width)),
                const((1, mine)),
                const((1, mine)),
            ],
            out_specs=[
                per(length, width),
                per(length, mine),
                per(length, mine),
                per(length, mine),
                per(heads, length, length),
                per(length, mine),
                per(length, width),
                const((length, length)),
                const((8, LANES)),
            ],
        ),
        out_shape=[
            S((seqs, length, width), low),
            S((seqs, length, mine), low),
            S((seqs, length, mine), low),
            S((seqs, length, mine), low),
            S((seqs, heads, length, length), low),
            S((seqs, length, mine), low),
            S((seqs, length, width), low),
            S((length, length), low),
            S((8, LANES), full),
        ],
        name="attend",
    )(order, crop_len, keep_mask[:, None, :], tokens, wq, wk, wv, wo, bq[None], bv[None])


def attend_back_kernel(
    grads, compact, q_in, k_in, v_in, p_in, ctx_in, wq, wk, wv, wo, part_out, weight_out, qb_out, vb_out, weights, qb, vb
):
    b = pl.program_id(0)

    @pl.when(b == 0)
    def _():
        weights[...] = jnp.zeros_like(weights)
        qb[...] = jnp.zeros_like(qb)
        vb[...] = jnp.zeros_like(vb)

    scale = 1.0 / math.sqrt(HEAD)
    grad = grads[0]
    mine = wq.shape[1]
    query, keys, values = q_in[0], k_in[0], v_in[0]
    context_grad = dot(grad, wo[...], ((1,), (1,))).astype(low)
    query_grads, keys_grads, values_grads = [], [], []
    for h in range(mine // HEAD):
        span = slice(h * HEAD, (h + 1) * HEAD)
        probs = p_in[0, h]
        wide = probs.astype(full)
        probs_grad = dot(context_grad[:, span], values[:, span], ((1,), (1,)))
        inner = jnp.sum(wide * probs_grad, axis=1, keepdims=True)
        score_grad = (wide * (probs_grad - inner)).astype(low)
        query_grads.append((dot(score_grad, keys[:, span]) * scale).astype(low))
        keys_grads.append((dot(score_grad, query[:, span], ((0,), (0,))) * scale).astype(low))
        values_grads.append(dot(probs, context_grad[:, span], ((0,), (0,))).astype(low))
    query_grad = jnp.concatenate(query_grads, axis=1)
    keys_grad = jnp.concatenate(keys_grads, axis=1)
    values_grad = jnp.concatenate(values_grads, axis=1)
    every = jnp.concatenate([query_grad, keys_grad, values_grad], axis=1)
    weights[:, : 3 * mine] += dot(compact[0], every, ((0,), (0,)))
    weights[:, 3 * mine :] += dot(grad, ctx_in[0], ((0,), (0,)))
    qb[...] += jnp.sum(query_grad.astype(full), axis=0, keepdims=True)
    vb[...] += jnp.sum(values_grad.astype(full), axis=0, keepdims=True)
    back = dot(query_grad, wq[...], ((1,), (1,)))
    back += dot(keys_grad, wk[...], ((1,), (1,)))
    back += dot(values_grad, wv[...], ((1,), (1,)))
    part_out[0] = back.astype(low)

    @pl.when(b == pl.num_programs(0) - 1)
    def _():
        weight_out[...] = weights[...].astype(low)
        qb_out[...] = qb[...]
        vb_out[...] = vb[...]


def attend_back(grads, compact, query, keys, values, probs, context, wq, wk, wv, wo):
    seqs, length, width = grads.shape
    mine = wq.shape[1]
    heads = mine // HEAD

    def const(shape):
        return pl.BlockSpec(shape, lambda b: (0,) * len(shape))

    def per(*shape):
        return pl.BlockSpec((1, *shape), lambda b: (b,) + (0,) * len(shape))

    S = jax.ShapeDtypeStruct
    return pl.pallas_call(
        attend_back_kernel,
        grid=(seqs,),
        in_specs=[
            per(length, width),
            per(length, width),
            per(length, mine),
            per(length, mine),
            per(length, mine),
            per(heads, length, length),
            per(length, mine),
            const((width, mine)),
            const((width, mine)),
            const((width, mine)),
            const((mine, width)),
        ],
        out_specs=[
            per(length, width),
            const((width, 4 * mine)),
            const((1, mine)),
            const((1, mine)),
        ],
        out_shape=[
            S((seqs, length, width), low),
            S((width, 4 * mine), low),
            S((1, mine), full),
            S((1, mine), full),
        ],
        scratch_shapes=[
            pltpu.VMEM((width, 4 * mine), full),
            pltpu.VMEM((1, mine), full),
            pltpu.VMEM((1, mine), full),
        ],
        name="attend_back",
    )(grads, compact, query, keys, values, probs, context, wq, wk, wv, wo)


def contrast(pooled, key_queue):
    width = pooled.shape[1]
    queries = jnp.concatenate([pooled, swap(pooled, "fsdp", 1)])
    for stride in strides("dp"):
        queries = jnp.concatenate([queries, swap(queries, "dp", stride)])
    logits = dot(queries, key_queue, ((1,), (1,))) * inv_temp
    top = jnp.max(logits, axis=1, keepdims=True)
    expo = jnp.exp(logits - top)
    total = jnp.sum(expo, axis=1, keepdims=True)
    rows = dot(expo.astype(low), key_queue)
    state = jnp.concatenate([rows, jnp.broadcast_to(top, (top.shape[0], LANES)), jnp.broadcast_to(total, (top.shape[0], LANES))], axis=1)
    for axis, stride in [("dp", s) for s in reversed(strides("dp"))] + [("fsdp", 1)]:
        half = state.shape[0] // 2
        kept, other = state[:half], swap(state[half:], axis, stride)
        top = jnp.maximum(kept[:, width : width + 1], other[:, width : width + 1])
        summed = kept * jnp.exp(kept[:, width : width + 1] - top) + other * jnp.exp(other[:, width : width + 1] - top)
        state = jnp.concatenate([summed[:, :width], jnp.broadcast_to(top, (half, LANES)), summed[:, width + LANES :]], axis=1)
    return (state[:, width : width + 1], state[:, width + LANES : width + LANES + 1], state[:, :width])


def own_positive(pos_keys, pos_index, group, member):
    share = pos_keys.shape[0]
    everything = jnp.concatenate([pos_keys, swap(pos_keys, "fsdp", 1)])
    for stride in strides("dp"):
        everything = jnp.concatenate([everything, swap(everything, "dp", stride)])
    place = lax.dynamic_index_in_dim(pos_index, group * share + member, 0, keepdims=False)
    row = ((place // share) ^ group) * share + place % share
    return lax.dynamic_slice_in_dim(everything, row, 1, 0).astype(full)


def per_device(
    tokens,
    keep_mask,
    crop_len,
    pos_index,
    pos_keys,
    key_queue,
    query_weight,
    query_bias,
    key_weight,
    value_weight,
    value_bias,
    out_weight,
    out_bias,
    norm_gain,
    norm_shift,
    up_weight,
    up_bias,
    down_weight,
    down_bias,
    final_gain,
    final_shift,
):
    seqs, length, width = tokens.shape
    assert seqs == 4 and lax.axis_size("tensor") == 4 and lax.axis_size("fsdp") == 2
    member = lax.axis_index("tensor")
    group = lax.axis_index(("dp", "fsdp"))
    devices = seqs * lax.axis_size("dp") * lax.axis_size("fsdp")
    mine = query_weight.shape[1]
    hidden = up_weight.shape[1]
    order = (member ^ jnp.array(RELATIVE, jnp.int32)).astype(jnp.int32)

    positive = own_positive(pos_keys, pos_index, group, member)
    compact, query, keys, values, probs, context, partial_out, table, counts = attend(
        tokens, keep_mask, crop_len, order, query_weight, key_weight, value_weight, out_weight, query_bias, value_bias
    )
    count = counts[0:1, 0:1]
    live = (jnp.arange(length, dtype=jnp.int32)[:, None].astype(full) < count).astype(full)
    normed_one, rstd_one = norm_parts(compact[0].astype(full) + tensor_sum(partial_out) + out_bias)
    middle = normed_one * norm_gain + norm_shift
    middle_all = tensor_gather(middle.astype(low)).reshape(seqs * length, width)
    pre = dot(middle_all, up_weight) + up_bias
    hidden_state, slope = gelu_parts(pre)
    hidden_state = hidden_state.astype(low)
    partial_ffn = dot(hidden_state, down_weight).astype(low).reshape(seqs, length, width)
    normed_two, rstd_two = norm_parts(middle + tensor_sum(partial_ffn) + down_bias)
    output = (normed_two * final_gain + final_shift).astype(low)
    live_sum = jnp.sum(normed_two * live, axis=0, keepdims=True)
    pooled = (live_sum / count * final_gain + final_shift).astype(low)

    pos_logit = jnp.sum(pooled.astype(full) * positive, axis=1, keepdims=True) * inv_temp
    top, total, key_sum = contrast(pooled, key_queue)
    top_final = jnp.maximum(top, pos_logit)
    lse = top_final + jnp.log(total * jnp.exp(top - top_final) + jnp.exp(pos_logit - top_final))
    loss_part = lse - pos_logit
    step = loss_scale * inv_temp
    pooled_grad = key_sum * (step * jnp.exp(top - lse)) + step * (jnp.exp(pos_logit - lse) - 1.0) * positive

    result_row = pooled_grad / count
    two_grad = norm_backward(result_row * final_gain * live, normed_two, rstd_two)
    final_gain_part = result_row * live_sum
    ffn_grad = two_grad.astype(low)
    down_bias_part = jnp.sum(ffn_grad.astype(full), axis=0, keepdims=True)
    ffn_grads = tensor_gather(ffn_grad).reshape(seqs * length, width)
    pre_grad = (slope * dot(ffn_grads, down_weight, ((1,), (1,)))).astype(low)
    back_part = dot(pre_grad, up_weight, ((1,), (1,))).astype(low).reshape(seqs, length, width)
    middle_grad = two_grad + tensor_sum(back_part)
    one_grad = norm_backward(middle_grad * norm_gain, normed_one, rstd_one)
    attn_grad = one_grad.astype(low)
    attn_grads = tensor_gather(attn_grad)
    down_weight_grad = group_sum(dot(hidden_state, ffn_grads, ((0,), (0,))).astype(low))
    up_weight_grad = group_sum(dot(middle_all, pre_grad, ((0,), (0,))).astype(low))
    up_bias_part = jnp.sum(pre_grad.astype(full), axis=0, keepdims=True)
    norm_gain_part = jnp.sum(middle_grad * normed_one, axis=0, keepdims=True)
    norm_shift_part = jnp.sum(middle_grad, axis=0, keepdims=True)
    out_bias_part = jnp.sum(attn_grad.astype(full), axis=0, keepdims=True)

    partial_in, attn_weight_grad, query_bias_part, value_bias_part = attend_back(
        attn_grads, compact, query, keys, values, probs, context, query_weight, key_weight, value_weight, out_weight
    )
    attn_weight_grad = group_sum(attn_weight_grad).astype(full)
    compact_grad = (one_grad + tensor_sum(partial_in)).astype(low)
    input_grad = dot(table, compact_grad, ((0,), (0,))).astype(low)

    vectors = jnp.concatenate(
        [
            final_gain_part,
            pooled_grad,
            norm_gain_part,
            norm_shift_part,
            down_bias_part,
            out_bias_part,
            jnp.broadcast_to(loss_part / devices, (1, width)),
        ]
    )
    vectors = lax.optimization_barrier(vectors)
    for stride in (1, 2):
        vectors = vectors + swap(vectors, "tensor", stride)
    pad = jnp.zeros((1, width - 2 * mine), full)
    narrow = jnp.concatenate([query_bias_part, value_bias_part, pad], axis=1)
    vectors = jnp.concatenate([vectors, narrow, up_bias_part.reshape(-1, width)])
    vectors = vectors + swap(vectors, "fsdp", 1)
    for stride in strides("dp"):
        vectors = vectors + swap(vectors, "dp", stride)
    return (
        output[None],
        input_grad[None],
        attn_weight_grad[:, :mine],
        vectors[7, :mine],
        attn_weight_grad[:, mine : 2 * mine],
        attn_weight_grad[:, 2 * mine : 3 * mine],
        vectors[7, mine : 2 * mine],
        attn_weight_grad[:, 3 * mine :].T,
        vectors[5],
        vectors[2],
        vectors[3],
        up_weight_grad.astype(full),
        vectors[8:].reshape(-1),
        down_weight_grad.astype(full),
        vectors[4],
        vectors[0],
        vectors[1],
        vectors[6, 0],
    )


def solution(mesh):
    placed = (
        P(("dp", "fsdp"), None, None),
        P(("dp", "fsdp"), None),
        P(("dp", "fsdp")),
        P(),
        P(("dp", "fsdp"), None),
        P(("dp", "fsdp"), None),
        P(None, "tensor"),
        P("tensor"),
        P(None, "tensor"),
        P(None, "tensor"),
        P("tensor"),
        P("tensor", None),
        P(),
        P(),
        P(),
        P(None, "tensor"),
        P("tensor"),
        P("tensor", None),
        P(),
        P(),
        P(),
    )
    return jax.shard_map(
        per_device,
        mesh=mesh,
        in_specs=placed,
        out_specs=(
            P(("dp", "fsdp", "tensor"), None, None),
            P(("dp", "fsdp", "tensor"), None, None),
            P(None, "tensor"),
            P("tensor"),
            P(None, "tensor"),
            P(None, "tensor"),
            P("tensor"),
            P("tensor", None),
            P(),
            P(),
            P(),
            P(None, "tensor"),
            P("tensor"),
            P("tensor", None),
            P(),
            P(),
            P(),
            P(),
        ),
        check_vma=False,
    )
```

```python
import math

import jax
import jax.numpy as jnp
from jax import lax
from jax.experimental import pallas as pl
from jax.experimental.pallas import tpu as pltpu
from jax.sharding import PartitionSpec as P

HEAD = 64
eps = 1e-12
inv_temp = 20.0
loss_scale = 256.0
low = jnp.bfloat16
full = jnp.float32
LANES = 128

RELATIVE = (0, 2, 1, 3)


def dot(a, b, dims=((1,), (0,))):
    return lax.dot_general(a, b, (dims, ((), ())), preferred_element_type=full)


def swap(array, axis, stride):
    size = lax.axis_size(axis)
    return lax.ppermute(array, axis, [(i, i ^ stride) for i in range(size)])


def strides(axis):
    size = lax.axis_size(axis)
    assert size & (size - 1) == 0
    return [1 << k for k in range(size.bit_length() - 1)]


def tensor_gather(block):
    pair = jnp.stack([block, swap(block, "tensor", 2)])
    return jnp.concatenate([pair, swap(pair, "tensor", 1)])


def tensor_sum(parts):
    other = swap(parts[2:], "tensor", 1)
    far = swap((parts[1].astype(full) + other[1].astype(full)).astype(low), "tensor", 2)
    return parts[0].astype(full) + other[0].astype(full) + far.astype(full)


def group_sum(grad):
    rows = grad.shape[0] // 2
    f = lax.axis_index("fsdp")
    kept = lax.dynamic_slice_in_dim(grad, f * rows, rows, 0)
    sent = lax.dynamic_slice_in_dim(grad, (1 - f) * rows, rows, 0)
    part = kept.astype(full) + swap(sent, "fsdp", 1).astype(full)
    if lax.axis_size("dp") == 4:
        z = lax.axis_index("dp")
        part = part + lax.ppermute(part.astype(low), "dp", [(0, 1), (3, 2)]).astype(full)
        part = part.astype(low)
        total = part.astype(full) + lax.ppermute(part, "dp", [(1, 2), (2, 1)]).astype(full)
        total = total.astype(low)
        outer = lax.ppermute(total, "dp", [(1, 0), (2, 3)])
        total = jnp.where((z == 0) | (z == 3), outer, total)
    else:
        total = lax.psum(part, "dp").astype(low)
    other = swap(total, "fsdp", 1)
    first = jnp.where(f == 0, total, other)
    second = jnp.where(f == 0, other, total)
    return jnp.concatenate([first, second])


def norm_parts(resid):
    center = resid - jnp.mean(resid, axis=-1, keepdims=True)
    rstd = lax.rsqrt(jnp.mean(center * center, axis=-1, keepdims=True) + eps)
    return (center * rstd, rstd)


def norm_backward(scaled, normed, rstd):
    inner = jnp.mean(scaled, axis=-1, keepdims=True)
    along = jnp.mean(scaled * normed, axis=-1, keepdims=True)
    return rstd * (scaled - inner - normed * along)


def gelu_parts(pre):
    cdf = 0.5 * (1.0 + lax.erf(pre * math.sqrt(0.5)))
    slope = cdf + pre * (jnp.exp(-0.5 * pre * pre) * (1.0 / math.sqrt(2.0 * math.pi)))
    return (pre * cdf, slope)


def attend_kernel(
    order, lens, mask, tokens, wq, wk, wv, wo, bq, bv, compact_out, q_out, k_out, v_out, p_out, ctx_out, part_out, table_out, count_out
):
    b = pl.program_id(0)
    length = mask.shape[-1]
    crop_len = lens[order[b]]
    lane = lax.broadcasted_iota(jnp.int32, (1, length), 1)
    kept = jnp.where(((mask[0] == 1) | (lane == 0)) & (lane < crop_len), 1.0, 0.0)
    rows = lax.broadcasted_iota(jnp.int32, (length, length), 0)
    cols = lax.broadcasted_iota(jnp.int32, (length, length), 1)
    upto = jnp.where(rows <= cols, 1.0, 0.0).astype(low)
    rank = dot(jnp.broadcast_to(kept, (8, length)).astype(low), upto)[0:1]
    place = jnp.where(kept > 0.0, rank - 1.0, -1.0)
    table = jnp.where(place == rows.astype(full), 1.0, 0.0).astype(low)
    count = jnp.sum(kept)

    @pl.when(b == 0)
    def _():
        table_out[...] = table
        count_out[...] = jnp.full(count_out.shape, count, full)

    compact = dot(table, tokens[0]).astype(low)
    compact_out[0] = compact
    query = (dot(compact, wq[...], ((1,), (1,))) + bq[...]).astype(low)
    keys = dot(compact, wk[...], ((1,), (1,))).astype(low)
    values = (dot(compact, wv[...], ((1,), (1,))) + bv[...]).astype(low)
    q_out[0], k_out[0], v_out[0] = query, keys, values
    live = lane.astype(full) < count
    contexts = []
    for h in range(query.shape[1] // HEAD):
        span = slice(h * HEAD, (h + 1) * HEAD)
        scores = dot(query[:, span], keys[:, span], ((1,), (1,))) * (1.0 / math.sqrt(HEAD))
        scores = jnp.where(live, scores, -1e30)
        expo = jnp.exp(scores - jnp.max(scores, axis=1, keepdims=True))
        probs = (expo / jnp.sum(expo, axis=1, keepdims=True)).astype(low)
        p_out[0, h] = probs
        contexts.append(dot(probs, values[:, span]).astype(low))
    context = jnp.concatenate(contexts, axis=1)
    ctx_out[0] = context
    part_out[0] = dot(context, wo[...]).astype(low)


def attend(tokens, keep_mask, crop_len, order, wq, wk, wv, wo, bq, bv):
    seqs, length, width = tokens.shape
    mine = wq.shape[0]
    heads = mine // HEAD

    def const(shape):
        return pl.BlockSpec(shape, lambda b, *_: (0,) * len(shape))

    def per(*shape):
        return pl.BlockSpec((1, *shape), lambda b, *_: (b,) + (0,) * len(shape))

    def picked(*shape):
        return pl.BlockSpec((1, *shape), lambda b, order, lens: (order[b],) + (0,) * len(shape))

    S = jax.ShapeDtypeStruct
    return pl.pallas_call(
        attend_kernel,
        grid_spec=pltpu.PrefetchScalarGridSpec(
            num_scalar_prefetch=2,
            grid=(seqs,),
            in_specs=[
                picked(1, length),
                picked(length, width),
                const((mine, width)),
                const((mine, width)),
                const((mine, width)),
                const((mine, width)),
                const((1, mine)),
                const((1, mine)),
            ],
            out_specs=[
                per(length, width),
                per(length, mine),
                per(length, mine),
                per(length, mine),
                per(heads, length, length),
                per(length, mine),
                per(length, width),
                const((length, length)),
                const((8, LANES)),
            ],
        ),
        out_shape=[
            S((seqs, length, width), low),
            S((seqs, length, mine), low),
            S((seqs, length, mine), low),
            S((seqs, length, mine), low),
            S((seqs, heads, length, length), low),
            S((seqs, length, mine), low),
            S((seqs, length, width), low),
            S((length, length), low),
            S((8, LANES), full),
        ],
        name="attend",
    )(order, crop_len, keep_mask[:, None, :], tokens, wq, wk, wv, wo, bq[None], bv[None])


def attend_back_kernel(
    grads, compact, q_in, k_in, v_in, p_in, ctx_in, wq, wk, wv, wo, part_out, weight_out, qb_out, vb_out, weights, qb, vb
):
    b = pl.program_id(0)

    @pl.when(b == 0)
    def _():
        weights[...] = jnp.zeros_like(weights)
        qb[...] = jnp.zeros_like(qb)
        vb[...] = jnp.zeros_like(vb)

    scale = 1.0 / math.sqrt(HEAD)
    grad = grads[0]
    mine = wq.shape[0]
    query, keys, values = q_in[0], k_in[0], v_in[0]
    context_grad = dot(grad, wo[...], ((1,), (1,))).astype(low)
    query_grads, keys_grads, values_grads = [], [], []
    for h in range(mine // HEAD):
        span = slice(h * HEAD, (h + 1) * HEAD)
        probs = p_in[0, h]
        wide = probs.astype(full)
        probs_grad = dot(context_grad[:, span], values[:, span], ((1,), (1,)))
        inner = jnp.sum(wide * probs_grad, axis=1, keepdims=True)
        score_grad = (wide * (probs_grad - inner)).astype(low)
        query_grads.append((dot(score_grad, keys[:, span]) * scale).astype(low))
        keys_grads.append((dot(score_grad, query[:, span], ((0,), (0,))) * scale).astype(low))
        values_grads.append(dot(probs, context_grad[:, span], ((0,), (0,))).astype(low))
    query_grad = jnp.concatenate(query_grads, axis=1)
    keys_grad = jnp.concatenate(keys_grads, axis=1)
    values_grad = jnp.concatenate(values_grads, axis=1)
    every = jnp.concatenate([query_grad, keys_grad, values_grad], axis=1)
    weights[: 3 * mine] += dot(every, compact[0], ((0,), (0,)))
    weights[3 * mine :] += dot(ctx_in[0], grad, ((0,), (0,)))
    qb[...] += jnp.sum(query_grad.astype(full), axis=0, keepdims=True)
    vb[...] += jnp.sum(values_grad.astype(full), axis=0, keepdims=True)
    back = dot(query_grad, wq[...])
    back += dot(keys_grad, wk[...])
    back += dot(values_grad, wv[...])
    part_out[0] = back.astype(low)

    @pl.when(b == pl.num_programs(0) - 1)
    def _():
        weight_out[...] = weights[...].astype(low)
        qb_out[...] = qb[...]
        vb_out[...] = vb[...]


def attend_back(grads, compact, query, keys, values, probs, context, wq, wk, wv, wo):
    seqs, length, width = grads.shape
    mine = wq.shape[0]
    heads = mine // HEAD

    def const(shape):
        return pl.BlockSpec(shape, lambda b: (0,) * len(shape))

    def per(*shape):
        return pl.BlockSpec((1, *shape), lambda b: (b,) + (0,) * len(shape))

    S = jax.ShapeDtypeStruct
    return pl.pallas_call(
        attend_back_kernel,
        grid=(seqs,),
        in_specs=[
            per(length, width),
            per(length, width),
            per(length, mine),
            per(length, mine),
            per(length, mine),
            per(heads, length, length),
            per(length, mine),
            const((mine, width)),
            const((mine, width)),
            const((mine, width)),
            const((mine, width)),
        ],
        out_specs=[
            per(length, width),
            const((4 * mine, width)),
            const((1, mine)),
            const((1, mine)),
        ],
        out_shape=[
            S((seqs, length, width), low),
            S((4 * mine, width), low),
            S((1, mine), full),
            S((1, mine), full),
        ],
        scratch_shapes=[
            pltpu.VMEM((4 * mine, width), full),
            pltpu.VMEM((1, mine), full),
            pltpu.VMEM((1, mine), full),
        ],
        name="attend_back",
    )(grads, compact, query, keys, values, probs, context, wq, wk, wv, wo)


def gather_feedforward(up_weight, up_bias, down_weight):
    f = lax.axis_index("fsdp")
    half = up_weight.shape[1] // 2
    up_y = swap(lax.dynamic_slice_in_dim(up_weight, f * half, half, 1), "tensor", 2)
    down_y = swap(lax.dynamic_slice_in_dim(down_weight, f * half, half, 0), "tensor", 2)
    up_x = swap(up_y, "fsdp", 1)
    down_x = swap(down_y, "fsdp", 1)
    bias = up_bias[None]
    bias = jnp.concatenate([bias, swap(bias, "tensor", 2)])
    bias = jnp.concatenate([bias, swap(bias, "tensor", 1)])
    blocks = []
    for base, other in ((0, False), (2, True)):
        across = (lambda a: swap(a, "tensor", 1)) if other else (lambda a: a)
        far = bias[base + 1 : base + 2]
        bias_y = lax.dynamic_slice_in_dim(far, f * half, half, 1)
        bias_x = lax.dynamic_slice_in_dim(far, (1 - f) * half, half, 1)
        blocks.append((across(up_weight), bias[base : base + 1], across(down_weight)))
        blocks.append((across(up_y), bias_y, across(down_y)))
        blocks.append((across(up_x), bias_x, across(down_x)))
    return [blocks[i] for i in (0, 3, 1, 4, 2, 5)]


def contrast(pooled, key_queue):
    width = pooled.shape[1]
    queries = jnp.concatenate([pooled, swap(pooled, "fsdp", 1)])
    for stride in strides("dp"):
        queries = jnp.concatenate([queries, swap(queries, "dp", stride)])
    logits = dot(queries, key_queue, ((1,), (1,))) * inv_temp
    top = jnp.max(logits, axis=1, keepdims=True)
    expo = jnp.exp(logits - top)
    total = jnp.sum(expo, axis=1, keepdims=True)
    rows = dot(expo.astype(low), key_queue)
    state = jnp.concatenate([rows, jnp.broadcast_to(top, (top.shape[0], LANES)), jnp.broadcast_to(total, (top.shape[0], LANES))], axis=1)
    for axis, stride in [("dp", s) for s in reversed(strides("dp"))] + [("fsdp", 1)]:
        half = state.shape[0] // 2
        kept, other = state[:half], swap(state[half:], axis, stride)
        top = jnp.maximum(kept[:, width : width + 1], other[:, width : width + 1])
        summed = kept * jnp.exp(kept[:, width : width + 1] - top) + other * jnp.exp(other[:, width : width + 1] - top)
        state = jnp.concatenate([summed[:, :width], jnp.broadcast_to(top, (half, LANES)), summed[:, width + LANES :]], axis=1)
    return (state[:, width : width + 1], state[:, width + LANES : width + LANES + 1], state[:, :width])


def own_positive(pos_keys, pos_index, group, member):
    share = pos_keys.shape[0]
    everything = jnp.concatenate([pos_keys, swap(pos_keys, "fsdp", 1)])
    for stride in strides("dp"):
        everything = jnp.concatenate([everything, swap(everything, "dp", stride)])
    place = lax.dynamic_index_in_dim(pos_index, group * share + member, 0, keepdims=False)
    row = ((place // share) ^ group) * share + place % share
    return lax.dynamic_slice_in_dim(everything, row, 1, 0).astype(full)


def per_device(
    tokens,
    keep_mask,
    crop_len,
    pos_index,
    pos_keys,
    key_queue,
    query_weight,
    query_bias,
    key_weight,
    value_weight,
    value_bias,
    out_weight,
    out_bias,
    norm_gain,
    norm_shift,
    up_weight,
    up_bias,
    down_weight,
    down_bias,
    final_gain,
    final_shift,
):
    seqs, length, width = tokens.shape
    assert seqs == 4 and lax.axis_size("tensor") == 4 and lax.axis_size("fsdp") == 2
    member = lax.axis_index("tensor")
    group = lax.axis_index(("dp", "fsdp"))
    devices = seqs * lax.axis_size("dp") * lax.axis_size("fsdp")
    mine = query_weight.shape[1]
    order = (member ^ jnp.array(RELATIVE, jnp.int32)).astype(jnp.int32)

    positive = own_positive(pos_keys, pos_index, group, member)
    blocks = gather_feedforward(up_weight, up_bias, down_weight)
    compact, query, keys, values, probs, context, partial_out, table, counts = attend(
        tokens, keep_mask, crop_len, order, query_weight.T, key_weight.T, value_weight.T, out_weight, query_bias, value_bias
    )
    count = counts[0:1, 0:1]
    live = (jnp.arange(length, dtype=jnp.int32)[:, None].astype(full) < count).astype(full)
    attn_out, positive = lax.optimization_barrier((tensor_sum(partial_out), positive))
    normed_one, rstd_one = norm_parts(compact[0].astype(full) + attn_out + out_bias)
    middle = normed_one * norm_gain + norm_shift
    middle_low = middle.astype(low)
    ffn_out = middle + down_bias
    slopes = []
    for up, bias, down in blocks:
        hidden_part, slope_part = gelu_parts(dot(middle_low, up) + bias)
        slopes.append(slope_part.astype(low))
        ffn_out = ffn_out + dot(hidden_part.astype(low), down)
    normed_two, rstd_two = norm_parts(ffn_out)
    output = (normed_two * final_gain + final_shift).astype(low)
    live_sum = jnp.sum(normed_two * live, axis=0, keepdims=True)
    pooled = (live_sum / count * final_gain + final_shift).astype(low)

    middle_all = tensor_gather(middle_low).reshape(seqs * length, width)
    hidden_state, slope = gelu_parts(dot(middle_all, up_weight) + up_bias)
    hidden_state = hidden_state.astype(low)

    pos_logit = jnp.sum(pooled.astype(full) * positive, axis=1, keepdims=True) * inv_temp
    top, total, key_sum = contrast(pooled, key_queue)
    top_final = jnp.maximum(top, pos_logit)
    lse = top_final + jnp.log(total * jnp.exp(top - top_final) + jnp.exp(pos_logit - top_final))
    loss_part = lse - pos_logit
    step = loss_scale * inv_temp
    pooled_grad = key_sum * (step * jnp.exp(top - lse)) + step * (jnp.exp(pos_logit - lse) - 1.0) * positive

    result_row = pooled_grad / count
    two_grad = norm_backward(result_row * final_gain * live, normed_two, rstd_two)
    final_gain_part = result_row * live_sum
    ffn_grad = two_grad.astype(low)
    down_bias_part = jnp.sum(ffn_grad.astype(full), axis=0, keepdims=True)
    middle_grad = two_grad
    for (up, _, down), slope_part in zip(blocks, slopes):
        grad_part = (slope_part.astype(full) * dot(ffn_grad, down, ((1,), (1,)))).astype(low)
        middle_grad = middle_grad + dot(grad_part, up, ((1,), (1,)))
    one_grad = norm_backward(middle_grad * norm_gain, normed_one, rstd_one)
    attn_grad = one_grad.astype(low)
    attn_grads = tensor_gather(attn_grad)
    ffn_grads = tensor_gather(ffn_grad).reshape(seqs * length, width)
    pre_grad = (slope * dot(ffn_grads, down_weight, ((1,), (1,)))).astype(low)
    down_weight_grad = group_sum(dot(hidden_state, ffn_grads, ((0,), (0,))).astype(low))
    up_weight_grad = group_sum(dot(middle_all, pre_grad, ((0,), (0,))).astype(low))
    up_bias_part = jnp.sum(pre_grad.astype(full), axis=0, keepdims=True)
    norm_gain_part = jnp.sum(middle_grad * normed_one, axis=0, keepdims=True)
    norm_shift_part = jnp.sum(middle_grad, axis=0, keepdims=True)
    out_bias_part = jnp.sum(attn_grad.astype(full), axis=0, keepdims=True)

    partial_in, attn_weight_grad, query_bias_part, value_bias_part = attend_back(
        attn_grads, compact, query, keys, values, probs, context, query_weight.T, key_weight.T, value_weight.T, out_weight
    )
    attn_weight_grad = group_sum(attn_weight_grad).astype(full)
    compact_grad = (one_grad + tensor_sum(partial_in)).astype(low)
    input_grad = dot(table, compact_grad, ((0,), (0,))).astype(low)

    vectors = jnp.concatenate(
        [
            final_gain_part,
            pooled_grad,
            norm_gain_part,
            norm_shift_part,
            down_bias_part,
            out_bias_part,
            jnp.broadcast_to(loss_part / devices, (1, width)),
        ]
    )
    vectors = lax.optimization_barrier(vectors)
    for stride in (1, 2):
        vectors = vectors + swap(vectors, "tensor", stride)
    pad = jnp.zeros((1, width - 2 * mine), full)
    narrow = jnp.concatenate([query_bias_part, value_bias_part, pad], axis=1)
    vectors = jnp.concatenate([vectors, narrow, up_bias_part.reshape(-1, width)])
    vectors = vectors + swap(vectors, "fsdp", 1)
    for stride in strides("dp"):
        vectors = vectors + swap(vectors, "dp", stride)
    return (
        output[None],
        input_grad[None],
        attn_weight_grad[:mine].T,
        vectors[7, :mine],
        attn_weight_grad[mine : 2 * mine].T,
        attn_weight_grad[2 * mine : 3 * mine].T,
        vectors[7, mine : 2 * mine],
        attn_weight_grad[3 * mine :],
        vectors[5],
        vectors[2],
        vectors[3],
        up_weight_grad.astype(full),
        vectors[8:].reshape(-1),
        down_weight_grad.astype(full),
        vectors[4],
        vectors[0],
        vectors[1],
        vectors[6, 0],
    )


def solution(mesh):
    placed = (
        P(("dp", "fsdp"), None, None),
        P(("dp", "fsdp"), None),
        P(("dp", "fsdp")),
        P(),
        P(("dp", "fsdp"), None),
        P(("dp", "fsdp"), None),
        P(None, "tensor"),
        P("tensor"),
        P(None, "tensor"),
        P(None, "tensor"),
        P("tensor"),
        P("tensor", None),
        P(),
        P(),
        P(),
        P(None, "tensor"),
        P("tensor"),
        P("tensor", None),
        P(),
        P(),
        P(),
    )
    return jax.shard_map(
        per_device,
        mesh=mesh,
        in_specs=placed,
        out_specs=(
            P(("dp", "fsdp", "tensor"), None, None),
            P(("dp", "fsdp", "tensor"), None, None),
            P(None, "tensor"),
            P("tensor"),
            P(None, "tensor"),
            P(None, "tensor"),
            P("tensor"),
            P("tensor", None),
            P(),
            P(),
            P(),
            P(None, "tensor"),
            P("tensor"),
            P("tensor", None),
            P(),
            P(),
            P(),
            P(),
        ),
        check_vma=False,
    )
```

```python
import math

import jax
import jax.numpy as jnp
from jax import lax
from jax.experimental import pallas as pl
from jax.experimental.pallas import tpu as pltpu
from jax.sharding import PartitionSpec as P

HEAD = 64
eps = 1e-12
inv_temp = 20.0
loss_scale = 256.0
low = jnp.bfloat16
full = jnp.float32
LANES = 128


def dot(a, b, dims=((1,), (0,))):
    return lax.dot_general(a, b, (dims, ((), ())), preferred_element_type=full)


def swap(array, axis, stride):
    size = lax.axis_size(axis)
    return lax.ppermute(array, axis, [(i, i ^ stride) for i in range(size)])


def strides(axis):
    size = lax.axis_size(axis)
    assert size & (size - 1) == 0
    return [1 << k for k in range(size.bit_length() - 1)]


def plus(part, other):
    return (part.astype(full) + other.astype(full)).astype(low)


def carried(rows):
    high = lax.reduce_precision(rows, 8, 7)
    return jnp.concatenate([high, rows - high]).astype(low)


def plus_carried(part, other, rows):
    ends = [a[rows:].astype(full) for a in (part, other)]
    count = ends[0].shape[0] // 2
    total = sum(e[:count] + e[count:] for e in ends)
    return jnp.concatenate([plus(part[:rows], other[:rows]), carried(total)])


def inward(part):
    return lax.ppermute(part, "dp", [(0, 1), (3, 2)])


def across(part):
    return lax.ppermute(part, "dp", [(1, 2), (2, 1)])


def outward(part):
    z = lax.axis_index("dp")
    outer = lax.ppermute(part, "dp", [(1, 0), (2, 3)])
    return jnp.where((z == 0) | (z == 3), outer, part)


def ordered(total, other, f):
    return (jnp.where(f == 0, total, other), jnp.where(f == 0, other, total))


def norm_parts(resid):
    center = resid - jnp.mean(resid, axis=-1, keepdims=True)
    rstd = lax.rsqrt(jnp.mean(center * center, axis=-1, keepdims=True) + eps)
    return (center * rstd, rstd)


def norm_backward(scaled, normed, rstd):
    inner = jnp.mean(scaled, axis=-1, keepdims=True)
    along = jnp.mean(scaled * normed, axis=-1, keepdims=True)
    return rstd * (scaled - inner - normed * along)


def gelu_parts(pre):
    cdf = 0.5 * (1.0 + lax.erf(pre * math.sqrt(0.5)))
    slope = cdf + pre * (jnp.exp(-0.5 * pre * pre) * (1.0 / math.sqrt(2.0 * math.pi)))
    return (pre * cdf, slope)


def relative(b):
    return ((b & 1) << 1) | (b >> 1)


def attend_kernel(
    place_in, lens, mask, tokens, wq, wk, wv, wo, bq, bv, compact_out, q_out, k_out, v_out, p_out, ctx_out, near_out, away_out, table_out, count_out
):
    b = pl.program_id(0)
    crop = place_in[0] ^ relative(b)
    length = mask.shape[-1]
    crop_len = lens[crop]
    lane = lax.broadcasted_iota(jnp.int32, (1, length), 1)
    kept = jnp.where(((mask[pl.ds(crop, 1), :] == 1) | (lane == 0)) & (lane < crop_len), 1.0, 0.0)
    rows = lax.broadcasted_iota(jnp.int32, (length, length), 0)
    cols = lax.broadcasted_iota(jnp.int32, (length, length), 1)
    upto = jnp.where(rows <= cols, 1.0, 0.0).astype(low)
    rank = dot(jnp.broadcast_to(kept, (8, length)).astype(low), upto)[0:1]
    place = jnp.where(kept > 0.0, rank - 1.0, -1.0)
    table = jnp.where(place == rows.astype(full), 1.0, 0.0).astype(low)
    count = jnp.sum(kept)

    @pl.when(b == 0)
    def _():
        table_out[...] = table
        count_out[...] = jnp.full(count_out.shape, count, full)

    compact = dot(table, tokens[0]).astype(low)
    compact_out[0] = compact
    query = (dot(compact, wq[...], ((1,), (1,))) + bq[...]).astype(low)
    keys = dot(compact, wk[...], ((1,), (1,))).astype(low)
    values = (dot(compact, wv[...], ((1,), (1,))) + bv[...]).astype(low)
    q_out[0], k_out[0], v_out[0] = query, keys, values
    live = lane.astype(full) < count
    contexts = []
    for h in range(query.shape[1] // HEAD):
        span = slice(h * HEAD, (h + 1) * HEAD)
        scores = dot(query[:, span], keys[:, span], ((1,), (1,))) * (1.0 / math.sqrt(HEAD))
        scores = jnp.where(live, scores, -1e30)
        expo = jnp.exp(scores - jnp.max(scores, axis=1, keepdims=True))
        probs = (expo / jnp.sum(expo, axis=1, keepdims=True)).astype(low)
        p_out[0, h] = probs
        contexts.append(dot(probs, values[:, span]).astype(low))
    context = jnp.concatenate(contexts, axis=1)
    ctx_out[0] = context
    part = dot(context, wo[...]).astype(low)

    @pl.when(b < 2)
    def _():
        near_out[0] = part

    @pl.when(b >= 2)
    def _():
        away_out[0] = part


def attend(tokens, keep_mask, crop_len, place, wq, wk, wv, wo, bq, bv):
    seqs, length, width = tokens.shape
    mine = wq.shape[0]
    heads = mine // HEAD

    def const(*shape):
        return pl.BlockSpec(shape, lambda b, *_: (0,) * len(shape))

    def per(*shape):
        return pl.BlockSpec((1, *shape), lambda b, *_: (b,) + (0,) * len(shape))

    S = jax.ShapeDtypeStruct
    return pl.pallas_call(
        attend_kernel,
        grid_spec=pltpu.PrefetchScalarGridSpec(
            num_scalar_prefetch=2,
            grid=(seqs,),
            in_specs=[
                const(seqs, length),
                pl.BlockSpec((1, length, width), lambda b, place, lens: (place[0] ^ relative(b), 0, 0)),
                const(mine, width),
                const(mine, width),
                const(mine, width),
                const(mine, width),
                const(1, mine),
                const(1, mine),
            ],
            out_specs=[
                per(length, width),
                per(length, mine),
                per(length, mine),
                per(length, mine),
                per(heads, length, length),
                per(length, mine),
                pl.BlockSpec((1, length, width), lambda b, *_: (jnp.minimum(b, 1), 0, 0)),
                pl.BlockSpec((1, length, width), lambda b, *_: (jnp.maximum(b - 2, 0), 0, 0)),
                const(length, length),
                const(8, LANES),
            ],
        ),
        out_shape=[
            S((seqs, length, width), low),
            S((seqs, length, mine), low),
            S((seqs, length, mine), low),
            S((seqs, length, mine), low),
            S((seqs, heads, length, length), low),
            S((seqs, length, mine), low),
            S((2, length, width), low),
            S((2, length, width), low),
            S((length, length), low),
            S((8, LANES), full),
        ],
        name="attend",
    )(place, crop_len, keep_mask, tokens, wq, wk, wv, wo, bq[None], bv[None])


def attend_back_kernel(
    place, g0, g1, g2, g3, compact, q_in, k_in, v_in, p_in, ctx_in, wq, wk, wv, wo, near_out, away_out, *refs
):
    b = pl.program_id(0)
    qk_kept, qk_sent, vo_kept, vo_sent, qb_out, vb_out, grad_s, weights, qb, vb = refs

    @pl.when(b == 0)
    def _():
        weights[...] = jnp.zeros_like(weights)
        qb[...] = jnp.zeros_like(qb)
        vb[...] = jnp.zeros_like(vb)

    for i, g in enumerate((g0, g1, g2, g3)):

        @pl.when(b == i)
        def _(g=g):
            grad_s[...] = g[...]

    scale = 1.0 / math.sqrt(HEAD)
    grad = grad_s[...]
    mine = wq.shape[0]
    query, keys, values = q_in[0], k_in[0], v_in[0]
    context_grad = dot(grad, wo[...], ((1,), (1,))).astype(low)
    query_grads, keys_grads, values_grads = [], [], []
    for h in range(mine // HEAD):
        span = slice(h * HEAD, (h + 1) * HEAD)
        probs = p_in[0, h]
        wide = probs.astype(full)
        probs_grad = dot(context_grad[:, span], values[:, span], ((1,), (1,)))
        inner = jnp.sum(wide * probs_grad, axis=1, keepdims=True)
        score_grad = (wide * (probs_grad - inner)).astype(low)
        query_grads.append((dot(score_grad, keys[:, span]) * scale).astype(low))
        keys_grads.append((dot(score_grad, query[:, span], ((0,), (0,))) * scale).astype(low))
        values_grads.append(dot(probs, context_grad[:, span], ((0,), (0,))).astype(low))
    query_grad = jnp.concatenate(query_grads, axis=1)
    keys_grad = jnp.concatenate(keys_grads, axis=1)
    values_grad = jnp.concatenate(values_grads, axis=1)
    every = jnp.concatenate([query_grad, keys_grad, values_grad], axis=1)
    weights[: 3 * mine] += dot(every, compact[0], ((0,), (0,)))
    weights[3 * mine :] += dot(ctx_in[0], grad, ((0,), (0,)))
    qb[...] += jnp.sum(query_grad.astype(full), axis=0, keepdims=True)
    vb[...] += jnp.sum(values_grad.astype(full), axis=0, keepdims=True)
    back = dot(query_grad, wq[...])
    back += dot(keys_grad, wk[...])
    back += dot(values_grad, wv[...])

    @pl.when(b < 2)
    def _():
        near_out[0] = back.astype(low)

    @pl.when(b >= 2)
    def _():
        away_out[0] = back.astype(low)

    @pl.when(b == pl.num_programs(0) - 1)
    def _():
        f = place[1] >> 1
        for target, block in ((qk_kept, f), (qk_sent, 1 - f), (vo_kept, 2 + f), (vo_sent, 3 - f)):
            target[...] = weights[pl.ds(pl.multiple_of(block * mine, mine), mine), :].astype(low)
        qb_out[...] = qb[...]
        vb_out[...] = vb[...]


def attend_back(place, grads, compact, query, keys, values, probs, context, wq, wk, wv, wo):
    seqs, length, width = compact.shape
    mine = wq.shape[0]
    heads = mine // HEAD

    def const(*shape):
        return pl.BlockSpec(shape, lambda b, *_: (0,) * len(shape))

    def per(*shape):
        return pl.BlockSpec((1, *shape), lambda b, *_: (b,) + (0,) * len(shape))

    S = jax.ShapeDtypeStruct
    return pl.pallas_call(
        attend_back_kernel,
        grid_spec=pltpu.PrefetchScalarGridSpec(
            num_scalar_prefetch=1,
            grid=(seqs,),
            in_specs=[const(length, width)] * 4
            + [
                per(length, width),
                per(length, mine),
                per(length, mine),
                per(length, mine),
                per(heads, length, length),
                per(length, mine),
                const(mine, width),
                const(mine, width),
                const(mine, width),
                const(mine, width),
            ],
            out_specs=[
                pl.BlockSpec((1, length, width), lambda b, *_: (jnp.minimum(b, 1), 0, 0)),
                pl.BlockSpec((1, length, width), lambda b, *_: (jnp.maximum(b - 2, 0), 0, 0)),
                const(mine, width),
                const(mine, width),
                const(mine, width),
                const(mine, width),
                const(1, mine),
                const(1, mine),
            ],
            scratch_shapes=[
                pltpu.VMEM((length, width), low),
                pltpu.VMEM((4 * mine, width), full),
                pltpu.VMEM((1, mine), full),
                pltpu.VMEM((1, mine), full),
            ],
        ),
        out_shape=[S((2, length, width), low)] * 2 + [S((mine, width), low)] * 4 + [S((1, mine), full)] * 2,
        name="attend_back",
    )(place, *grads, compact, query, keys, values, probs, context, wq, wk, wv, wo)


WHOLE, QUARTERS = 4, 8


def weight_copies(place, wholes, quarters, up, down, sems):
    rows = quarters[0].shape[0] // 2
    shards = []
    for s in range(2):
        shards.append([(wholes[2 * s], up.at[s]), (wholes[2 * s + 1], down.at[s])])
    for s in range(2):
        copies = []
        for i, flip in enumerate((0, 2, 1, 3)):
            spot = pl.ds(pl.multiple_of((place[1] ^ flip) * rows, rows), rows)
            piece = quarters[4 * s + i]
            copies.append((piece.at[pl.ds(0, rows)], up.at[2 + s, spot]))
            copies.append((piece.at[pl.ds(rows, rows)], down.at[2 + s, spot]))
        shards.append(copies)
    number, made = 0, []
    for copies in shards:
        row = []
        for source, target in copies:
            row.append(pltpu.make_async_copy(source, target, sems.at[number]))
            number += 1
        made.append(row)
    return made


def ffn_kernel(place, *refs):
    wholes, quarters = refs[:WHOLE], refs[WHOLE : WHOLE + QUARTERS]
    middle, biases, down_bias, gain, shift, counts = refs[12:18]
    slopes_out, normed_out, rows_out, output_out, sums_out, pooled_out = refs[18:24]
    up, down, sems = refs[24:]
    shards = weight_copies(place, wholes, quarters, up, down, sems)
    for copies in shards:
        for copy in copies:
            copy.start()
    length, width = middle.shape
    mid = middle[...]
    mid_low = mid.astype(low)
    total = mid + down_bias[...]
    for s, copies in enumerate(shards):
        for copy in copies:
            copy.wait()
        hidden, slope = gelu_parts(dot(mid_low, up[s]) + biases[s : s + 1])
        slopes_out[s] = slope.astype(low)
        total += dot(hidden.astype(low), down[s])
    normed, rstd = norm_parts(total)
    normed_out[...] = normed
    output_out[0] = (normed * gain[...] + shift[...]).astype(low)
    count = counts[0:1, 0:1]
    live = jnp.where(lax.broadcasted_iota(jnp.int32, (length, 1), 0).astype(full) < count, 1.0, 0.0)
    factor = rstd * live
    rows_out[:, :width] = normed.astype(low)
    lane = lax.broadcasted_iota(jnp.int32, (length, LANES), 1)
    first = factor.astype(low).astype(full)
    rows_out[:, width:] = jnp.where(lane == 0, first, jnp.where(lane == 1, factor - first, 0.0)).astype(low)
    live_sum = jnp.sum(normed * live, axis=0, keepdims=True)
    sums_out[...] = live_sum
    pooled_out[:, :width] = (live_sum / count * gain[...] + shift[...]).astype(low)
    pooled_out[:, width:] = jnp.broadcast_to(count, (1, LANES)).astype(low)


def ffn_back_kernel(place, *refs):
    wholes, quarters = refs[:WHOLE], refs[WHOLE : WHOLE + QUARTERS]
    slopes, vector, normed_two, rows, normed_one, rstd_one, gain = refs[12:19]
    attn_out, one_out, sums_out = refs[19:22]
    up, down, sems = refs[22:]
    shards = weight_copies(place, wholes, quarters, up, down, sems)
    for copies in shards:
        for copy in copies:
            copy.start()
    length, width = normed_two.shape
    factor = rows[:, width : width + 1].astype(full) + rows[:, width + 1 : width + 2].astype(full)
    two_grad = norm_backward(jnp.broadcast_to(vector[...], (length, width)), normed_two[...], factor)
    ffn_grad = two_grad.astype(low)
    total = two_grad
    for s, copies in enumerate(shards):
        for copy in copies:
            copy.wait()
        grad = (slopes[s].astype(full) * dot(ffn_grad, down[s], ((1,), (1,)))).astype(low)
        total += dot(grad, up[s], ((1,), (1,)))
    normed = normed_one[...]
    one_grad = norm_backward(total * gain[...], normed, rstd_one[:, 0:1])
    one_out[...] = one_grad
    attn_grad = one_grad.astype(low)
    attn_out[...] = attn_grad
    sums_out[0:1] = jnp.sum(total * normed, axis=0, keepdims=True)
    sums_out[1:2] = jnp.sum(total, axis=0, keepdims=True)
    sums_out[2:3] = jnp.sum(ffn_grad.astype(full), axis=0, keepdims=True)
    sums_out[3:4] = jnp.sum(attn_grad.astype(full), axis=0, keepdims=True)
    sums_out[4:8] = jnp.zeros((4, width), full)


def with_weights(kernel, name, place, wholes, quarters, operands, outs):
    width, hidden = wholes[0].shape
    everywhere = pl.BlockSpec(memory_space=pl.ANY)
    return pl.pallas_call(
        kernel,
        grid_spec=pltpu.PrefetchScalarGridSpec(
            num_scalar_prefetch=1,
            grid=(1,),
            in_specs=[everywhere] * (WHOLE + QUARTERS)
            + [pl.BlockSpec(a.shape, lambda b, *_, rank=a.ndim: (0,) * rank) for a in operands],
            out_specs=[pl.BlockSpec(o.shape, lambda b, *_, rank=len(o.shape): (0,) * rank) for o in outs],
            scratch_shapes=[
                pltpu.VMEM((4, width, hidden), low),
                pltpu.VMEM((4, hidden, width), low),
                pltpu.SemaphoreType.DMA((20,)),
            ],
        ),
        out_shape=outs,
        name=name,
    )(place, *wholes, *quarters, *operands)


def ffn_weights_kernel(*refs):
    middles, rows = refs[:8], refs[8:16]
    vectors, up, bias, down = refs[16:20]
    down_out, up_out, bias_out = refs[20:]
    width = middles[0].shape[1]
    down_sum = up_sum = bias_sum = None
    for i in range(8):
        middle = middles[i][...]
        hidden, slope = gelu_parts(dot(middle, up[...]) + bias[...])
        normed = rows[i][:, :width].astype(full)
        factor = rows[i][:, width : width + 1].astype(full) + rows[i][:, width + 1 : width + 2].astype(full)
        vector = vectors[i : i + 1]
        along = jnp.mean(normed * vector, axis=1, keepdims=True)
        ffn_grad = (factor * ((vector - jnp.mean(vector, axis=1, keepdims=True)) - normed * along)).astype(low)
        pre_grad = (slope * dot(ffn_grad, down[...], ((1,), (1,)))).astype(low)
        one = dot(hidden.astype(low), ffn_grad, ((0,), (0,)))
        two = dot(middle, pre_grad, ((0,), (0,)))
        three = jnp.sum(pre_grad.astype(full), axis=0, keepdims=True)
        down_sum, up_sum, bias_sum = (one, two, three) if i == 0 else (down_sum + one, up_sum + two, bias_sum + three)
    down_out[...] = down_sum.astype(low)
    up_out[...] = up_sum.astype(low)
    bias_out[...] = bias_sum


def ffn_weights(middles, rows, vectors, up, bias, down):
    half, width = down.shape
    S = jax.ShapeDtypeStruct
    return pl.pallas_call(
        ffn_weights_kernel,
        out_shape=[S((half, width), low), S((width, half), low), S((1, half), full)],
        name="ffn_weights",
    )(*middles, *rows, vectors, up, bias, down)


def contrast(pooled, key_queue, gathered, returned):
    width = key_queue.shape[1]
    queries = jnp.concatenate([pooled, swap(pooled, "fsdp", 1)])
    both = queries
    queries = gathered(queries)
    for stride in strides("dp"):
        queries = jnp.concatenate([queries, swap(queries, "dp", stride)])
    logits = dot(queries[:, :width], key_queue, ((1,), (1,))) * inv_temp
    top = jnp.max(logits, axis=1, keepdims=True)
    expo = jnp.exp(logits - top)
    total = jnp.sum(expo, axis=1, keepdims=True)
    rows = dot(expo.astype(low), key_queue)
    state = jnp.concatenate([rows, jnp.broadcast_to(top, (top.shape[0], LANES)), jnp.broadcast_to(total, (top.shape[0], LANES))], axis=1)
    for axis, stride in [("dp", s) for s in reversed(strides("dp"))] + [("fsdp", 1)]:
        half = state.shape[0] // 2
        if axis == "fsdp":
            kept, other = state, swap(jnp.concatenate([state[1:2], state[0:1]]), axis, stride)
        else:
            if stride == 1:
                state = returned(state)
            kept, other = state[:half], swap(state[half:], axis, stride)
        top = jnp.maximum(kept[:, width : width + 1], other[:, width : width + 1])
        summed = kept * jnp.exp(kept[:, width : width + 1] - top) + other * jnp.exp(other[:, width : width + 1] - top)
        state = jnp.concatenate([summed[:, :width], jnp.broadcast_to(top, (top.shape[0], LANES)), summed[:, width + LANES :]], axis=1)
    return (state[:, width : width + 1], state[:, width + LANES : width + LANES + 1], state[:, :width], both)


def per_device(
    tokens,
    keep_mask,
    crop_len,
    pos_index,
    pos_keys,
    key_queue,
    query_weight,
    query_bias,
    key_weight,
    value_weight,
    value_bias,
    out_weight,
    out_bias,
    norm_gain,
    norm_shift,
    up_weight,
    up_bias,
    down_weight,
    down_bias,
    final_gain,
    final_shift,
):
    seqs, length, width = tokens.shape
    hidden = up_weight.shape[1]
    assert seqs == 4 and lax.axis_size("tensor") == 4 and lax.axis_size("fsdp") == 2 and hidden == width
    member = lax.axis_index("tensor")
    f = lax.axis_index("fsdp")
    z = lax.axis_index("dp")
    group = lax.axis_index(("dp", "fsdp"))
    devices = seqs * lax.axis_size("dp") * lax.axis_size("fsdp")
    mine = query_weight.shape[1]
    tie = lax.optimization_barrier
    kind = f * 2 + (z & 1)
    place = jnp.stack([member, kind]).astype(jnp.int32)
    quarter, half = hidden // 4, hidden // 2

    def quarter_of(which):
        return jnp.concatenate([lax.dynamic_slice_in_dim(w, which * quarter, quarter, 0) for w in (up_weight, down_weight)])

    piece_y = swap(quarter_of(kind), "tensor", 2)
    piece_d = swap(quarter_of(kind ^ 3), "tensor", 2)
    bias_pair = jnp.concatenate([up_bias[None], swap(up_bias[None], "tensor", 1)])
    biases = jnp.concatenate([bias_pair, swap(bias_pair, "tensor", 2)])
    wholes = [up_weight, down_weight, swap(up_weight, "tensor", 1), swap(down_weight, "tensor", 1)]
    up_half = lax.dynamic_slice_in_dim(up_weight, f * half, half, 1)
    down_half = lax.dynamic_slice_in_dim(down_weight, f * half, half, 0)
    bias_half = lax.dynamic_slice_in_dim(up_bias[None], f * half, half, 1)

    known = jnp.concatenate([pos_keys, swap(pos_keys, "fsdp", 1)])
    compact, query, keys, values, probs, context, near, away, table, counts = attend(
        tokens, keep_mask, crop_len, place, query_weight.T, key_weight.T, value_weight.T, out_weight, query_bias, value_bias
    )
    near, away, piece_y, known = tie((near, away, piece_y, known))
    other = swap(away, "tensor", 1)
    piece_x = swap(piece_y, "fsdp", 1)
    piece_z = swap(piece_y, "dp", 1)
    share = pos_keys.shape[0]
    spot = jnp.arange(devices, dtype=jnp.int32)[None]
    mates = jnp.stack([group, group ^ 1]) * share + member
    wanted = jnp.sum(jnp.where(spot == mates[:, None], pos_index[None], 0), axis=1, keepdims=True)
    chosen = jnp.where(((spot // share) ^ group) * share + spot % share == wanted, 1.0, 0.0).astype(low)
    sent, piece_d, biases, chosen = tie((plus(near[1], other[1]), piece_d, biases, chosen))
    hops = strides("dp")
    for stride in hops[:-1]:
        known = jnp.concatenate([known, swap(known, "dp", stride)])
    attn_out = near[0].astype(full) + other[0].astype(full) + swap(sent, "tensor", 2).astype(full)
    attn_out, piece_x, piece_z, known = tie((attn_out, piece_x, piece_z, known))

    normed_one, rstd_one = norm_parts(compact[0].astype(full) + attn_out + out_bias)
    rstd_one = jnp.broadcast_to(rstd_one, (length, LANES))
    middle = normed_one * norm_gain + norm_shift
    middle_low = middle.astype(low)
    quarters = [piece_y, piece_x, piece_z, piece_d]
    quarters = quarters + [swap(p, "tensor", 1) for p in quarters]
    S = jax.ShapeDtypeStruct
    slopes, normed_two, rows, output, live_sum, pooled = with_weights(
        ffn_kernel,
        "ffn",
        place,
        wholes,
        quarters,
        [middle, biases, down_bias[None], final_gain[None], final_shift[None], counts],
        [
            S((4, length, hidden), low),
            S((length, width), full),
            S((length, width + LANES), low),
            S((1, length, width), low),
            S((1, width), full),
            S((1, width + LANES), low),
        ],
    )

    middle_x, middle_y = swap(middle_low, "fsdp", 1), swap(middle_low, "tensor", 2)
    known = jnp.concatenate([known, swap(known, "dp", hops[-1])])
    pooled, middle_x, middle_y, known, rstd_one = tie((pooled, middle_x, middle_y, known, rstd_one))
    pairs = {}

    def gathered(queries):
        queries, row_own, mid = tie((queries, rows, middle_x))
        pairs["x"], pairs["y"] = swap(row_own, "fsdp", 1), swap(row_own, "tensor", 2)
        pairs["mid"] = swap(mid, "tensor", 2)
        return queries

    def returned(state):
        state, pairs["x"], pairs["y"], pairs["mid"] = tie((state, pairs["x"], pairs["y"], pairs["mid"]))
        return state

    positive = dot(chosen, known)
    top, total, key_sum, pooled_pair = contrast(pooled, key_queue, gathered, returned)
    count_pair = pooled_pair[:, width : width + 1].astype(full)
    middle_pair = [middle_low, middle_x, middle_y, pairs["mid"]]
    rows_pair = [rows, pairs["x"], pairs["y"], swap(pairs["x"], "tensor", 2)]
    middles = middle_pair + [swap(p, "tensor", 1) for p in middle_pair]
    rows_all = rows_pair + [swap(p, "tensor", 1) for p in rows_pair]

    pos_logit = jnp.sum(pooled_pair[:, :width].astype(full) * positive, axis=1, keepdims=True) * inv_temp
    top_final = jnp.maximum(top, pos_logit)
    lse = top_final + jnp.log(total * jnp.exp(top - top_final) + jnp.exp(pos_logit - top_final))
    loss_part = (lse - pos_logit)[0:1]
    step = loss_scale * inv_temp
    pooled_grad = key_sum * (step * jnp.exp(top - lse)) + step * (jnp.exp(pos_logit - lse) - 1.0) * positive
    result_row = pooled_grad / count_pair
    vector_pair = result_row * final_gain
    final_gain_part = result_row[0:1] * live_sum

    vectors_far = jnp.concatenate([vector_pair, swap(vector_pair, "tensor", 2)])
    vectors_all = jnp.concatenate([vectors_far, swap(vectors_far, "tensor", 1)])

    attn_grad, one_grad, sums = with_weights(
        ffn_back_kernel,
        "ffn_back",
        place,
        wholes,
        quarters,
        [slopes, vector_pair[0:1], normed_two, rows, normed_one, rstd_one, norm_gain[None]],
        [S((length, width), low), S((length, width), full), S((8, width), full)],
    )
    vectors_all, attn_grad, rows_all, middles = tie((vectors_all, attn_grad, rows_all, middles))
    down_part, up_part, up_bias_half = ffn_weights(middles, rows_all, vectors_all, up_half, bias_half, down_half)
    attn_far, attn_core, down_part, up_part = tie((swap(attn_grad, "tensor", 2), swap(attn_grad, "tensor", 1), down_part, up_part))
    attn_grads = [attn_grad, attn_far, attn_core, swap(attn_far, "tensor", 1)]

    near_in, away_in, qk_kept, qk_sent, vo_kept, vo_sent, query_bias_part, value_bias_part = attend_back(
        place, attn_grads, compact, query, keys, values, probs, context, query_weight.T, key_weight.T, value_weight.T, out_weight
    )
    line = lax.axis_size("dp") == 4
    down_next = inward(down_part) if line else down_part
    qk_sent, vo_sent, near_in, away_in, down_next = tie((qk_sent, vo_sent, near_in, away_in, down_next))
    qk_sum = plus(qk_kept, swap(qk_sent, "fsdp", 1))
    vectors = jnp.concatenate([final_gain_part, pooled_grad[0:1], sums[0:4], jnp.broadcast_to(loss_part / devices, (1, width))])
    vectors, _ = tie((vectors, qk_sent))
    for stride in (2, 1):
        vectors = vectors + swap(vectors, "tensor", stride)
    pad = jnp.zeros((1, width - 2 * mine), full)
    narrow = jnp.concatenate([query_bias_part, value_bias_part, pad], axis=1)
    blank = jnp.zeros_like(up_bias_half)
    up_bias_part = jnp.concatenate([jnp.where(f == 0, up_bias_half, blank), jnp.where(f == 0, blank, up_bias_half)], axis=1)
    vectors = jnp.concatenate([vectors, narrow, up_bias_part, jnp.zeros((7, width), full)])
    extra = carried(vectors)
    vo_sum = plus_carried(jnp.concatenate([vo_kept, extra]), swap(jnp.concatenate([vo_sent, extra]), "fsdp", 1), mine)
    if line:
        down_sum = plus(down_part, down_next)
        up_sum = plus(up_part, inward(up_part))
        qk_sum, up_sum = tie((qk_sum, up_sum))
        down_sum = plus(down_sum, across(down_sum))
        qk_sum = plus(qk_sum, inward(qk_sum))
        down_sum, vo_sum, qk_sum = tie((down_sum, vo_sum, qk_sum))
        up_sum = plus(up_sum, across(up_sum))
        vo_sum = plus_carried(vo_sum, inward(vo_sum), mine)
        up_sum, vo_sum = tie((up_sum, vo_sum))
        qk_sum = plus(qk_sum, across(qk_sum))
        down_sum = outward(down_sum)
        down_sum, qk_sum = tie((down_sum, qk_sum))
        vo_sum = plus_carried(vo_sum, across(vo_sum), mine)
        down_other = swap(down_sum, "fsdp", 1)
        up_sum = outward(up_sum)
        qk_sum = outward(qk_sum)
        up_sum, vo_sum = tie((up_sum, vo_sum))
        vo_sum = outward(vo_sum)
    else:
        down_sum, up_sum, qk_sum, vo_sum = [lax.psum(a.astype(full), "dp").astype(low) for a in (down_part, up_part, qk_sum, vo_sum)]
        down_other = swap(down_sum, "fsdp", 1)
    if line:
        extra = vo_sum[mine:].astype(full)
        vectors = extra[:16] + extra[16:]
    else:
        vectors = lax.psum(vectors + swap(vectors, "fsdp", 1), "dp")
    vo_sum = vo_sum[:mine]
    down_weight_grad = jnp.concatenate(ordered(down_sum, down_other, f)).astype(full)
    up_weight_grad = jnp.concatenate(ordered(up_sum, swap(up_sum, "fsdp", 1), f), axis=1).astype(full)
    query_grad, key_grad = ordered(qk_sum, swap(qk_sum, "fsdp", 1), f)
    value_grad, out_grad = ordered(vo_sum, swap(vo_sum, "fsdp", 1), f)

    other_in = swap(away_in, "tensor", 1)
    far_in = swap(plus(near_in[1], other_in[1]), "tensor", 2)
    back = near_in[0].astype(full) + other_in[0].astype(full) + far_in.astype(full)
    compact_grad = (one_grad + back).astype(low)
    input_grad = dot(table, compact_grad, ((0,), (0,))).astype(low)
    return (
        output,
        input_grad[None],
        query_grad.T.astype(full),
        vectors[7, :mine],
        key_grad.T.astype(full),
        value_grad.T.astype(full),
        vectors[7, mine : 2 * mine],
        out_grad.astype(full),
        vectors[5],
        vectors[2],
        vectors[3],
        up_weight_grad,
        vectors[8],
        down_weight_grad,
        vectors[4],
        vectors[0],
        vectors[1],
        vectors[6, 0],
    )


def solution(mesh):
    placed = (
        P(("dp", "fsdp"), None, None),
        P(("dp", "fsdp"), None),
        P(("dp", "fsdp")),
        P(),
        P(("dp", "fsdp"), None),
        P(("dp", "fsdp"), None),
        P(None, "tensor"),
        P("tensor"),
        P(None, "tensor"),
        P(None, "tensor"),
        P("tensor"),
        P("tensor", None),
        P(),
        P(),
        P(),
        P(None, "tensor"),
        P("tensor"),
        P("tensor", None),
        P(),
        P(),
        P(),
    )
    return jax.shard_map(
        per_device,
        mesh=mesh,
        in_specs=placed,
        out_specs=(
            P(("dp", "fsdp", "tensor"), None, None),
            P(("dp", "fsdp", "tensor"), None, None),
            P(None, "tensor"),
            P("tensor"),
            P(None, "tensor"),
            P(None, "tensor"),
            P("tensor"),
            P("tensor", None),
            P(),
            P(),
            P(),
            P(None, "tensor"),
            P("tensor"),
            P("tensor", None),
            P(),
            P(),
            P(),
            P(),
        ),
        check_vma=False,
    )
```

```python
import math

import jax
import jax.numpy as jnp
from jax import lax
from jax.experimental import pallas as pl
from jax.experimental.pallas import tpu as pltpu
from jax.sharding import PartitionSpec as P

HEAD = 64
eps = 1e-12
inv_temp = 20.0
loss_scale = 256.0
low = jnp.bfloat16
full = jnp.float32
LANES = 128


def dot(a, b, dims=((1,), (0,))):
    return lax.dot_general(a, b, (dims, ((), ())), preferred_element_type=full)


def swap(array, axis, stride):
    size = lax.axis_size(axis)
    return lax.ppermute(array, axis, [(i, i ^ stride) for i in range(size)])


def strides(axis):
    size = lax.axis_size(axis)
    assert size & (size - 1) == 0
    return [1 << k for k in range(size.bit_length() - 1)]


def plus(part, other):
    return (part.astype(full) + other.astype(full)).astype(low)


def carried(rows):
    high = lax.reduce_precision(rows, 8, 7)
    return jnp.concatenate([high, rows - high]).astype(low)


def plus_carried(part, other, rows):
    ends = [a[rows:].astype(full) for a in (part, other)]
    count = ends[0].shape[0] // 2
    total = sum(e[:count] + e[count:] for e in ends)
    return jnp.concatenate([plus(part[:rows], other[:rows]), carried(total)])


def inward(part):
    return lax.ppermute(part, "dp", [(0, 1), (3, 2)])


def across(part):
    return lax.ppermute(part, "dp", [(1, 2), (2, 1)])


def outward(part):
    z = lax.axis_index("dp")
    outer = lax.ppermute(part, "dp", [(1, 0), (2, 3)])
    return jnp.where((z == 0) | (z == 3), outer, part)


def ordered(total, other, f):
    return (jnp.where(f == 0, total, other), jnp.where(f == 0, other, total))


def norm_parts(resid):
    center = resid - jnp.mean(resid, axis=-1, keepdims=True)
    rstd = lax.rsqrt(jnp.mean(center * center, axis=-1, keepdims=True) + eps)
    return (center * rstd, rstd)


def norm_backward(scaled, normed, rstd):
    inner = jnp.mean(scaled, axis=-1, keepdims=True)
    along = jnp.mean(scaled * normed, axis=-1, keepdims=True)
    return rstd * (scaled - inner - normed * along)


def gelu_parts(pre):
    cdf = 0.5 * (1.0 + lax.erf(pre * math.sqrt(0.5)))
    slope = cdf + pre * (jnp.exp(-0.5 * pre * pre) * (1.0 / math.sqrt(2.0 * math.pi)))
    return (pre * cdf, slope)


def relative(b):
    return ((b & 1) << 1) | (b >> 1)


def attend_kernel(
    place_in, lens, mask, tokens, wq, wk, wv, wo, bq, bv, compact_out, q_out, k_out, v_out, p_out, ctx_out, near_out, away_out, table_out, count_out
):
    b = pl.program_id(0)
    crop = place_in[0] ^ relative(b)
    length = mask.shape[-1]
    crop_len = lens[crop]
    lane = lax.broadcasted_iota(jnp.int32, (1, length), 1)
    kept = jnp.where(((mask[pl.ds(crop, 1), :] == 1) | (lane == 0)) & (lane < crop_len), 1.0, 0.0)
    rows = lax.broadcasted_iota(jnp.int32, (length, length), 0)
    cols = lax.broadcasted_iota(jnp.int32, (length, length), 1)
    upto = jnp.where(rows <= cols, 1.0, 0.0).astype(low)
    rank = dot(jnp.broadcast_to(kept, (8, length)).astype(low), upto)[0:1]
    place = jnp.where(kept > 0.0, rank - 1.0, -1.0)
    table = jnp.where(place == rows.astype(full), 1.0, 0.0).astype(low)
    count = jnp.sum(kept)

    @pl.when(b == 0)
    def _():
        table_out[...] = table
        count_out[...] = jnp.full(count_out.shape, count, full)

    compact = dot(table, tokens[0]).astype(low)
    compact_out[0] = compact
    query = (dot(compact, wq[...], ((1,), (1,))) + bq[...]).astype(low)
    keys = dot(compact, wk[...], ((1,), (1,))).astype(low)
    values = (dot(compact, wv[...], ((1,), (1,))) + bv[...]).astype(low)
    q_out[0], k_out[0], v_out[0] = query, keys, values
    live = lane.astype(full) < count
    contexts = []
    for h in range(query.shape[1] // HEAD):
        span = slice(h * HEAD, (h + 1) * HEAD)
        scores = dot(query[:, span], keys[:, span], ((1,), (1,))) * (1.0 / math.sqrt(HEAD))
        scores = jnp.where(live, scores, -1e30)
        expo = jnp.exp(scores - jnp.max(scores, axis=1, keepdims=True))
        probs = (expo / jnp.sum(expo, axis=1, keepdims=True)).astype(low)
        p_out[0, h] = probs
        contexts.append(dot(probs, values[:, span]).astype(low))
    context = jnp.concatenate(contexts, axis=1)
    ctx_out[0] = context
    part = dot(context, wo[...]).astype(low)

    @pl.when(b < 2)
    def _():
        near_out[0] = part

    @pl.when(b >= 2)
    def _():
        away_out[0] = part


def attend(tokens, keep_mask, crop_len, place, wq, wk, wv, wo, bq, bv):
    seqs, length, width = tokens.shape
    mine = wq.shape[0]
    heads = mine // HEAD

    def const(*shape):
        return pl.BlockSpec(shape, lambda b, *_: (0,) * len(shape))

    def per(*shape):
        return pl.BlockSpec((1, *shape), lambda b, *_: (b,) + (0,) * len(shape))

    S = jax.ShapeDtypeStruct
    return pl.pallas_call(
        attend_kernel,
        grid_spec=pltpu.PrefetchScalarGridSpec(
            num_scalar_prefetch=2,
            grid=(seqs,),
            in_specs=[
                const(seqs, length),
                pl.BlockSpec((1, length, width), lambda b, place, lens: (place[0] ^ relative(b), 0, 0)),
                const(mine, width),
                const(mine, width),
                const(mine, width),
                const(mine, width),
                const(1, mine),
                const(1, mine),
            ],
            out_specs=[
                per(length, width),
                per(length, mine),
                per(length, mine),
                per(length, mine),
                per(heads, length, length),
                per(length, mine),
                pl.BlockSpec((1, length, width), lambda b, *_: (jnp.minimum(b, 1), 0, 0)),
                pl.BlockSpec((1, length, width), lambda b, *_: (jnp.maximum(b - 2, 0), 0, 0)),
                const(length, length),
                const(8, LANES),
            ],
        ),
        out_shape=[
            S((seqs, length, width), low),
            S((seqs, length, mine), low),
            S((seqs, length, mine), low),
            S((seqs, length, mine), low),
            S((seqs, heads, length, length), low),
            S((seqs, length, mine), low),
            S((2, length, width), low),
            S((2, length, width), low),
            S((length, length), low),
            S((8, LANES), full),
        ],
        name="attend",
    )(place, crop_len, keep_mask, tokens, wq, wk, wv, wo, bq[None], bv[None])


def attend_back_kernel(
    place, g0, g1, g2, g3, compact, q_in, k_in, v_in, p_in, ctx_in, wq, wk, wv, wo, near_out, away_out, *refs
):
    b = pl.program_id(0)
    qk_kept, qk_sent, vo_kept, vo_sent, qb_out, vb_out, grad_s, weights, qb, vb = refs

    @pl.when(b == 0)
    def _():
        weights[...] = jnp.zeros_like(weights)
        qb[...] = jnp.zeros_like(qb)
        vb[...] = jnp.zeros_like(vb)

    for i, g in enumerate((g0, g1, g2, g3)):

        @pl.when(b == i)
        def _(g=g):
            grad_s[...] = g[...]

    scale = 1.0 / math.sqrt(HEAD)
    grad = grad_s[...]
    mine = wq.shape[0]
    query, keys, values = q_in[0], k_in[0], v_in[0]
    context_grad = dot(grad, wo[...], ((1,), (1,))).astype(low)
    query_grads, keys_grads, values_grads = [], [], []
    for h in range(mine // HEAD):
        span = slice(h * HEAD, (h + 1) * HEAD)
        probs = p_in[0, h]
        wide = probs.astype(full)
        probs_grad = dot(context_grad[:, span], values[:, span], ((1,), (1,)))
        inner = jnp.sum(wide * probs_grad, axis=1, keepdims=True)
        score_grad = (wide * (probs_grad - inner)).astype(low)
        query_grads.append((dot(score_grad, keys[:, span]) * scale).astype(low))
        keys_grads.append((dot(score_grad, query[:, span], ((0,), (0,))) * scale).astype(low))
        values_grads.append(dot(probs, context_grad[:, span], ((0,), (0,))).astype(low))
    query_grad = jnp.concatenate(query_grads, axis=1)
    keys_grad = jnp.concatenate(keys_grads, axis=1)
    values_grad = jnp.concatenate(values_grads, axis=1)
    every = jnp.concatenate([query_grad, keys_grad, values_grad], axis=1)
    weights[: 3 * mine] += dot(every, compact[0], ((0,), (0,)))
    weights[3 * mine :] += dot(ctx_in[0], grad, ((0,), (0,)))
    qb[...] += jnp.sum(query_grad.astype(full), axis=0, keepdims=True)
    vb[...] += jnp.sum(values_grad.astype(full), axis=0, keepdims=True)
    back = dot(query_grad, wq[...])
    back += dot(keys_grad, wk[...])
    back += dot(values_grad, wv[...])

    @pl.when(b < 2)
    def _():
        near_out[0] = back.astype(low)

    @pl.when(b >= 2)
    def _():
        away_out[0] = back.astype(low)

    @pl.when(b == pl.num_programs(0) - 1)
    def _():
        f = place[1] >> 1
        for target, block in ((qk_kept, f), (qk_sent, 1 - f), (vo_kept, 2 + f), (vo_sent, 3 - f)):
            target[...] = weights[pl.ds(pl.multiple_of(block * mine, mine), mine), :].astype(low)
        qb_out[...] = qb[...]
        vb_out[...] = vb[...]


def attend_back(place, grads, compact, query, keys, values, probs, context, wq, wk, wv, wo):
    seqs, length, width = compact.shape
    mine = wq.shape[0]
    heads = mine // HEAD

    def const(*shape):
        return pl.BlockSpec(shape, lambda b, *_: (0,) * len(shape))

    def per(*shape):
        return pl.BlockSpec((1, *shape), lambda b, *_: (b,) + (0,) * len(shape))

    S = jax.ShapeDtypeStruct
    return pl.pallas_call(
        attend_back_kernel,
        grid_spec=pltpu.PrefetchScalarGridSpec(
            num_scalar_prefetch=1,
            grid=(seqs,),
            in_specs=[const(length, width)] * 4
            + [
                per(length, width),
                per(length, mine),
                per(length, mine),
                per(length, mine),
                per(heads, length, length),
                per(length, mine),
                const(mine, width),
                const(mine, width),
                const(mine, width),
                const(mine, width),
            ],
            out_specs=[
                pl.BlockSpec((1, length, width), lambda b, *_: (jnp.minimum(b, 1), 0, 0)),
                pl.BlockSpec((1, length, width), lambda b, *_: (jnp.maximum(b - 2, 0), 0, 0)),
                const(mine, width),
                const(mine, width),
                const(mine, width),
                const(mine, width),
                const(1, mine),
                const(1, mine),
            ],
            scratch_shapes=[
                pltpu.VMEM((length, width), low),
                pltpu.VMEM((4 * mine, width), full),
                pltpu.VMEM((1, mine), full),
                pltpu.VMEM((1, mine), full),
            ],
        ),
        out_shape=[S((2, length, width), low)] * 2 + [S((mine, width), low)] * 4 + [S((1, mine), full)] * 2,
        name="attend_back",
    )(place, *grads, compact, query, keys, values, probs, context, wq, wk, wv, wo)


WHOLE, QUARTERS = 4, 6


def weight_copies(place, wholes, quarters, up, down, sems):
    rows = quarters[0].shape[0] // 4
    shards = []
    for s in range(2):
        shards.append([(wholes[2 * s], up.at[s]), (wholes[2 * s + 1], down.at[s])])
    for s in range(2):
        copies = []
        for i, flip, start in ((0, 0, 0), (1, 2, 0), (2, 1, 0), (0, 3, 2)):
            spot = pl.ds(pl.multiple_of((place[1] ^ flip) * rows, rows), rows)
            piece = quarters[3 * s + i]
            copies.append((piece.at[pl.ds(start * rows, rows)], up.at[2 + s, spot]))
            copies.append((piece.at[pl.ds((start + 1) * rows, rows)], down.at[2 + s, spot]))
        shards.append(copies)
    number, made = 0, []
    for copies in shards:
        row = []
        for source, target in copies:
            row.append(pltpu.make_async_copy(source, target, sems.at[number]))
            number += 1
        made.append(row)
    return made


def ffn_kernel(place, *refs):
    wholes, quarters = refs[:WHOLE], refs[WHOLE : WHOLE + QUARTERS]
    middle, biases, affine, counts = refs[10:14]
    slopes_out, normed_out, rows_out, output_out, sums_out, pooled_out = refs[14:20]
    up, down, sems = refs[20:]
    down_bias, gain, shift = affine[0:1], affine[1:2], affine[2:3]
    shards = weight_copies(place, wholes, quarters, up, down, sems)
    for copies in shards[:2]:
        for copy in copies:
            copy.start()
    length, width = middle.shape
    mid = middle[...]
    mid_low = mid.astype(low)
    total = mid + down_bias
    for s, copies in enumerate(shards):
        for copy in copies:
            copy.wait()
        for copy in shards[s + 2] if s < 2 else []:
            copy.start()
        hidden, slope = gelu_parts(dot(mid_low, up[s]) + biases[s : s + 1])
        slopes_out[s] = slope.astype(low)
        total += dot(hidden.astype(low), down[s])
    normed, rstd = norm_parts(total)
    normed_out[...] = normed
    output_out[0] = (normed * gain + shift).astype(low)
    count = counts[0:1, 0:1]
    live = jnp.where(lax.broadcasted_iota(jnp.int32, (length, 1), 0).astype(full) < count, 1.0, 0.0)
    factor = rstd * live
    rows_out[:, :width] = normed.astype(low)
    lane = lax.broadcasted_iota(jnp.int32, (length, LANES), 1)
    first = factor.astype(low).astype(full)
    rows_out[:, width:] = jnp.where(lane == 0, first, jnp.where(lane == 1, factor - first, 0.0)).astype(low)
    live_sum = jnp.sum(normed * live, axis=0, keepdims=True)
    sums_out[...] = live_sum
    pooled_out[:, :width] = (live_sum / count * gain + shift).astype(low)
    pooled_out[:, width:] = jnp.broadcast_to(count, (1, LANES)).astype(low)


def ffn_back_kernel(place, *refs):
    wholes, quarters = refs[:WHOLE], refs[WHOLE : WHOLE + QUARTERS]
    slopes, vector, normed_two, rows, summed, affine = refs[10:16]
    attn_out, one_out, sums_out = refs[16:19]
    up, down, sems = refs[19:]
    shards = weight_copies(place, wholes, quarters, up, down, sems)
    for copies in shards[:2]:
        for copy in copies:
            copy.start()
    length, width = normed_two.shape
    factor = rows[:, width : width + 1].astype(full) + rows[:, width + 1 : width + 2].astype(full)
    two_grad = norm_backward(jnp.broadcast_to(vector[...], (length, width)), normed_two[...], factor)
    ffn_grad = two_grad.astype(low)
    total = two_grad
    for s, copies in enumerate(shards):
        for copy in copies:
            copy.wait()
        for copy in shards[s + 2] if s < 2 else []:
            copy.start()
        grad = (slopes[s].astype(full) * dot(ffn_grad, down[s], ((1,), (1,)))).astype(low)
        total += dot(grad, up[s], ((1,), (1,)))
    normed, rstd = norm_parts(summed[...])
    one_grad = norm_backward(total * affine[3:4], normed, rstd)
    one_out[...] = one_grad
    attn_grad = one_grad.astype(low)
    attn_out[...] = attn_grad
    sums_out[0:1] = jnp.sum(total * normed, axis=0, keepdims=True)
    sums_out[1:2] = jnp.sum(total, axis=0, keepdims=True)
    sums_out[2:3] = jnp.sum(ffn_grad.astype(full), axis=0, keepdims=True)
    sums_out[3:4] = jnp.sum(attn_grad.astype(full), axis=0, keepdims=True)
    sums_out[4:8] = jnp.zeros((4, width), full)


def with_weights(kernel, name, place, wholes, quarters, operands, outs):
    width, hidden = wholes[0].shape
    everywhere = pl.BlockSpec(memory_space=pl.ANY)
    return pl.pallas_call(
        kernel,
        grid_spec=pltpu.PrefetchScalarGridSpec(
            num_scalar_prefetch=1,
            grid=(1,),
            in_specs=[everywhere] * (WHOLE + QUARTERS)
            + [pl.BlockSpec(a.shape, lambda b, *_, rank=a.ndim: (0,) * rank) for a in operands],
            out_specs=[pl.BlockSpec(o.shape, lambda b, *_, rank=len(o.shape): (0,) * rank) for o in outs],
            scratch_shapes=[
                pltpu.VMEM((4, width, hidden), low),
                pltpu.VMEM((4, hidden, width), low),
                pltpu.SemaphoreType.DMA((20,)),
            ],
        ),
        out_shape=outs,
        name=name,
    )(place, *wholes, *quarters, *operands)


def ffn_weights_kernel(*refs):
    middles, rows = refs[:8], refs[8:16]
    vectors, up, bias, down = refs[16:20]
    down_out, up_out, bias_out = refs[20:]
    width = middles[0].shape[1]
    down_sum = up_sum = bias_sum = None
    for i in range(8):
        middle = middles[i][...]
        hidden, slope = gelu_parts(dot(middle, up[...]) + bias[...])
        normed = rows[i][:, :width].astype(full)
        factor = rows[i][:, width : width + 1].astype(full) + rows[i][:, width + 1 : width + 2].astype(full)
        vector = vectors[i : i + 1]
        along = jnp.mean(normed * vector, axis=1, keepdims=True)
        ffn_grad = (factor * ((vector - jnp.mean(vector, axis=1, keepdims=True)) - normed * along)).astype(low)
        pre_grad = (slope * dot(ffn_grad, down[...], ((1,), (1,)))).astype(low)
        one = dot(hidden.astype(low), ffn_grad, ((0,), (0,)))
        two = dot(middle, pre_grad, ((0,), (0,)))
        three = jnp.sum(pre_grad.astype(full), axis=0, keepdims=True)
        down_sum, up_sum, bias_sum = (one, two, three) if i == 0 else (down_sum + one, up_sum + two, bias_sum + three)
    down_out[...] = down_sum.astype(low)
    up_out[...] = up_sum.astype(low)
    bias_out[...] = bias_sum


def ffn_weights(middles, rows, vectors, up, bias, down):
    half, width = down.shape
    S = jax.ShapeDtypeStruct
    return pl.pallas_call(
        ffn_weights_kernel,
        out_shape=[S((half, width), low), S((width, half), low), S((1, half), full)],
        name="ffn_weights",
    )(*middles, *rows, vectors, up, bias, down)


def contrast(pooled, key_queue, gathered, halfway, returned):
    width = key_queue.shape[1]
    queries = jnp.concatenate([pooled, swap(pooled, "fsdp", 1)])
    both = queries
    queries = gathered(queries)
    for stride in strides("dp"):
        queries = jnp.concatenate([queries, swap(queries, "dp", stride)])
    queries = halfway(queries)
    logits = dot(queries[:, :width], key_queue, ((1,), (1,))) * inv_temp
    top = jnp.max(logits, axis=1, keepdims=True)
    expo = jnp.exp(logits - top)
    total = jnp.sum(expo, axis=1, keepdims=True)
    rows = dot(expo.astype(low), key_queue)
    state = jnp.concatenate([rows, jnp.broadcast_to(top, (top.shape[0], LANES)), jnp.broadcast_to(total, (top.shape[0], LANES))], axis=1)
    for axis, stride in [("dp", s) for s in reversed(strides("dp"))] + [("fsdp", 1)]:
        half = state.shape[0] // 2
        if axis == "fsdp":
            state = returned(state)
            kept, other = state, swap(jnp.concatenate([state[1:2], state[0:1]]), axis, stride)
        else:
            kept, other = state[:half], swap(state[half:], axis, stride)
        top = jnp.maximum(kept[:, width : width + 1], other[:, width : width + 1])
        summed = kept * jnp.exp(kept[:, width : width + 1] - top) + other * jnp.exp(other[:, width : width + 1] - top)
        state = jnp.concatenate([summed[:, :width], jnp.broadcast_to(top, (top.shape[0], LANES)), summed[:, width + LANES :]], axis=1)
    return (state[:, width : width + 1], state[:, width + LANES : width + LANES + 1], state[:, :width], both)


def per_device(
    tokens,
    keep_mask,
    crop_len,
    pos_index,
    pos_keys,
    key_queue,
    query_weight,
    query_bias,
    key_weight,
    value_weight,
    value_bias,
    out_weight,
    out_bias,
    norm_gain,
    norm_shift,
    up_weight,
    up_bias,
    down_weight,
    down_bias,
    final_gain,
    final_shift,
):
    seqs, length, width = tokens.shape
    hidden = up_weight.shape[1]
    assert seqs == 4 and lax.axis_size("tensor") == 4 and lax.axis_size("fsdp") == 2 and hidden == width
    member = lax.axis_index("tensor")
    f = lax.axis_index("fsdp")
    z = lax.axis_index("dp")
    group = lax.axis_index(("dp", "fsdp"))
    devices = seqs * lax.axis_size("dp") * lax.axis_size("fsdp")
    mine = query_weight.shape[1]
    tie = lax.optimization_barrier
    kind = f * 2 + (z & 1)
    place = jnp.stack([member, kind]).astype(jnp.int32)
    quarter, half = hidden // 4, hidden // 2

    def quarter_of(which):
        return [lax.dynamic_slice_in_dim(w, which * quarter, quarter, 0) for w in (up_weight, down_weight)]

    piece_y = swap(jnp.concatenate(quarter_of(kind) + quarter_of(kind ^ 3)), "tensor", 2)
    wholes = [up_weight, down_weight, swap(up_weight, "tensor", 1), swap(down_weight, "tensor", 1)]
    up_half = lax.dynamic_slice_in_dim(up_weight, f * half, half, 1)
    down_half = lax.dynamic_slice_in_dim(down_weight, f * half, half, 0)
    bias_half = lax.dynamic_slice_in_dim(up_bias[None], f * half, half, 1)

    known = jnp.concatenate([pos_keys, swap(pos_keys, "fsdp", 1)])
    compact, query, keys, values, probs, context, near, away, table, counts = attend(
        tokens, keep_mask, crop_len, place, query_weight.T, key_weight.T, value_weight.T, out_weight, query_bias, value_bias
    )
    affine = jnp.stack([down_bias, final_gain, final_shift, norm_gain])
    for stride in strides("dp"):
        known = jnp.concatenate([known, swap(known, "dp", stride)])
    compact, piece_y, known, wholes, affine, up_half, down_half, bias_half = tie(
        (compact, piece_y, known, wholes, affine, up_half, down_half, bias_half)
    )
    other = swap(away, "tensor", 1)
    share = pos_keys.shape[0]
    spot = jnp.arange(devices, dtype=jnp.int32)[None]
    mates = jnp.stack([group, group ^ 1]) * share + member
    wanted = jnp.sum(jnp.where(spot == mates[:, None], pos_index[None], 0), axis=1, keepdims=True)
    chosen = jnp.where(((spot // share) ^ group) * share + spot % share == wanted, 1.0, 0.0).astype(low)
    sent, piece_y, bias_own = tie((plus(near[1], other[1]), piece_y, up_bias))
    bias_far = swap(bias_own[None], "tensor", 2)
    first = piece_y[: 2 * quarter]
    piece_x = swap(first, "fsdp", 1)
    piece_z = swap(first, "dp", 1)
    bias_pair = jnp.concatenate([up_bias[None], bias_far])
    bias_pair = jnp.concatenate([bias_pair, swap(bias_pair, "tensor", 1)])
    biases = jnp.stack([bias_pair[0], bias_pair[2], bias_pair[1], bias_pair[3]])
    attn_out = near[0].astype(full) + other[0].astype(full) + swap(sent, "tensor", 2).astype(full)
    quarters = [piece_y, piece_x, piece_z]
    quarters = quarters + [swap(p, "tensor", 1) for p in quarters]

    summed = compact[0].astype(full) + attn_out + out_bias
    middle = norm_parts(summed)[0] * norm_gain + norm_shift
    middle_low = middle.astype(low)
    quarters, biases, chosen, middle, middle_low = tie((quarters, biases, chosen, middle, middle_low))
    S = jax.ShapeDtypeStruct
    slopes, normed_two, rows, output, live_sum, pooled = with_weights(
        ffn_kernel,
        "ffn",
        place,
        wholes,
        quarters,
        [middle, biases, affine, counts],
        [
            S((4, length, hidden), low),
            S((length, width), full),
            S((length, width + LANES), low),
            S((1, length, width), low),
            S((1, width), full),
            S((1, width + LANES), low),
        ],
    )

    middle_x, middle_y = swap(middle_low, "fsdp", 1), swap(middle_low, "tensor", 2)
    pooled, middle_x, middle_y = tie((pooled, middle_x, middle_y))
    pairs = {}

    def gathered(queries):
        queries, row_own, mid = tie((queries, rows, middle_x))
        pairs["x"], pairs["y"] = swap(row_own, "fsdp", 1), swap(row_own, "tensor", 2)
        pairs["mid"] = swap(mid, "tensor", 2)
        return queries

    def halfway(queries):
        queries, pairs["mid"] = tie((queries, pairs["mid"]))
        return queries

    def returned(state):
        state, pairs["x"], pairs["y"] = tie((state, pairs["x"], pairs["y"]))
        return state

    positive = dot(chosen, known)
    top, total, key_sum, pooled_pair = contrast(pooled, key_queue, gathered, halfway, returned)
    count_pair = pooled_pair[:, width : width + 1].astype(full)
    middle_pair = [middle_low, middle_x, middle_y, pairs["mid"]]
    rows_pair = [rows, pairs["x"], pairs["y"]]
    middles = middle_pair + [swap(p, "tensor", 1) for p in middle_pair]
    rows_core = [swap(p, "tensor", 1) for p in rows_pair]

    pos_logit = jnp.sum(pooled_pair[:, :width].astype(full) * positive, axis=1, keepdims=True) * inv_temp
    top_final = jnp.maximum(top, pos_logit)
    lse = top_final + jnp.log(total * jnp.exp(top - top_final) + jnp.exp(pos_logit - top_final))
    loss_part = (lse - pos_logit)[0:1]
    step = loss_scale * inv_temp
    pooled_grad = key_sum * (step * jnp.exp(top - lse)) + step * (jnp.exp(pos_logit - lse) - 1.0) * positive
    result_row = pooled_grad / count_pair
    vector_pair = result_row * final_gain
    final_gain_part = result_row[0:1] * live_sum

    vector_pair, rows_core = tie((vector_pair, rows_core))
    attn_grad, one_grad, sums = with_weights(
        ffn_back_kernel,
        "ffn_back",
        place,
        wholes,
        quarters,
        [slopes, vector_pair[0:1], normed_two, rows, summed, affine],
        [S((length, width), low), S((length, width), full), S((8, width), full)],
    )
    vectors_far, rows_far, attn_grad, middles, sums = tie((swap(vector_pair, "tensor", 2), swap(pairs["x"], "tensor", 2), attn_grad, middles, sums))
    vectors_far = jnp.concatenate([vector_pair, vectors_far])
    vectors_all = jnp.concatenate([vectors_far, swap(vectors_far, "tensor", 1)])
    rows_all = rows_pair + [rows_far] + rows_core + [swap(rows_far, "tensor", 1)]
    vectors = jnp.concatenate([final_gain_part, pooled_grad[0:1], sums[0:4], jnp.broadcast_to(loss_part / devices, (1, width))])
    down, up, up_bias_half = ffn_weights(middles, rows_all, vectors_all, up_half, bias_half, down_half)
    vectors = vectors + swap(vectors, "tensor", 1)
    attn_far, attn_core, down, up, vectors = tie((swap(attn_grad, "tensor", 2), swap(attn_grad, "tensor", 1), down, up, vectors))
    attn_grads = [attn_grad, attn_far, attn_core, swap(attn_far, "tensor", 1)]

    near_in, away_in, qk_kept, qk_sent, vo_kept, vo_sent, query_bias_part, value_bias_part = attend_back(
        place, attn_grads, compact, query, keys, values, probs, context, query_weight.T, key_weight.T, value_weight.T, out_weight
    )
    line = lax.axis_size("dp") == 4
    moved = inward(down) if line else down
    qk_sent, vo_sent, near_in, away_in, moved, vectors = tie((qk_sent, vo_sent, near_in, away_in, moved, vectors))
    vectors = vectors + swap(vectors, "tensor", 2)
    pad = jnp.zeros((1, width - 2 * mine), full)
    narrow = jnp.concatenate([query_bias_part, value_bias_part, pad], axis=1)
    blank = jnp.zeros_like(up_bias_half)
    up_bias_part = jnp.concatenate([jnp.where(f == 0, up_bias_half, blank), jnp.where(f == 0, blank, up_bias_half)], axis=1)
    vectors = jnp.concatenate([vectors, narrow, up_bias_part, jnp.zeros((7, width), full)])
    extra = carried(vectors)
    if line:
        up_in = inward(up)
        qk = plus(qk_kept, swap(qk_sent, "fsdp", 1))
        vo = plus_carried(jnp.concatenate([vo_kept, extra]), swap(jnp.concatenate([vo_sent, extra]), "fsdp", 1), mine)
        down = plus(down, moved)
        down = plus(down, across(down))
        qk, up_in = tie((qk, up_in))
        up = plus(up, up_in)
        vo, down = tie((vo, down))
        qk = plus(qk, inward(qk))
        vo = plus_carried(vo, inward(vo), mine)
        up = plus(up, across(up))
        up, vo = tie((up, vo))
        qk = plus(qk, across(qk))
        down = outward(down)
        qk, down = tie((qk, down))
        vo = plus_carried(vo, across(vo), mine)
        up = outward(up)
        qk = outward(qk)
        vo = outward(vo)
        extra, vo = vo[mine:].astype(full), vo[:mine]
        vectors = extra[:16] + extra[16:]
    else:
        down, up, qk, vo = [
            lax.psum(a.astype(full), "dp").astype(low)
            for a in (down, up, plus(qk_kept, swap(qk_sent, "fsdp", 1)), plus(vo_kept, swap(vo_sent, "fsdp", 1)))
        ]
        vectors = lax.psum(vectors + swap(vectors, "fsdp", 1), "dp")
    down_other, up_other, qk_other, vo_other = [swap(a, "fsdp", 1) for a in (down, up, qk, vo)]
    down_weight_grad = jnp.concatenate(ordered(down, down_other, f)).astype(full)
    up_weight_grad = jnp.concatenate(ordered(up, up_other, f), axis=1).astype(full)
    query_grad, key_grad = ordered(qk, qk_other, f)
    value_grad, out_grad = ordered(vo, vo_other, f)

    other_in = swap(away_in, "tensor", 1)
    far_in = swap(plus(near_in[1], other_in[1]), "tensor", 2)
    back = near_in[0].astype(full) + other_in[0].astype(full) + far_in.astype(full)
    compact_grad = (one_grad + back).astype(low)
    input_grad = dot(table, compact_grad, ((0,), (0,))).astype(low)
    return (
        output,
        input_grad[None],
        query_grad.T.astype(full),
        vectors[7, :mine],
        key_grad.T.astype(full),
        value_grad.T.astype(full),
        vectors[7, mine : 2 * mine],
        out_grad.astype(full),
        vectors[5],
        vectors[2],
        vectors[3],
        up_weight_grad,
        vectors[8],
        down_weight_grad,
        vectors[4],
        vectors[0],
        vectors[1],
        vectors[6, 0],
    )


def solution(mesh):
    placed = (
        P(("dp", "fsdp"), None, None),
        P(("dp", "fsdp"), None),
        P(("dp", "fsdp")),
        P(),
        P(("dp", "fsdp"), None),
        P(("dp", "fsdp"), None),
        P(None, "tensor"),
        P("tensor"),
        P(None, "tensor"),
        P(None, "tensor"),
        P("tensor"),
        P("tensor", None),
        P(),
        P(),
        P(),
        P(None, "tensor"),
        P("tensor"),
        P("tensor", None),
        P(),
        P(),
        P(),
    )
    return jax.shard_map(
        per_device,
        mesh=mesh,
        in_specs=placed,
        out_specs=(
            P(("dp", "fsdp", "tensor"), None, None),
            P(("dp", "fsdp", "tensor"), None, None),
            P(None, "tensor"),
            P("tensor"),
            P(None, "tensor"),
            P(None, "tensor"),
            P("tensor"),
            P("tensor", None),
            P(),
            P(),
            P(),
            P(None, "tensor"),
            P("tensor"),
            P("tensor", None),
            P(),
            P(),
            P(),
            P(),
        ),
        check_vma=False,
    )
```

```python
import math

import jax
import jax.numpy as jnp
from jax import lax
from jax.experimental import pallas as pl
from jax.experimental.pallas import tpu as pltpu
from jax.sharding import PartitionSpec as P

HEAD = 64
eps = 1e-12
inv_temp = 20.0
loss_scale = 256.0
low = jnp.bfloat16
full = jnp.float32
LANES = 128


def dot(a, b, dims=((1,), (0,))):
    return lax.dot_general(a, b, (dims, ((), ())), preferred_element_type=full)


def swap(array, axis, stride):
    size = lax.axis_size(axis)
    return lax.ppermute(array, axis, [(i, i ^ stride) for i in range(size)])


def strides(axis):
    size = lax.axis_size(axis)
    assert size & (size - 1) == 0
    return [1 << k for k in range(size.bit_length() - 1)]


def plus(part, other):
    return (part.astype(full) + other.astype(full)).astype(low)


def carried(rows):
    high = lax.reduce_precision(rows, 8, 7)
    return jnp.concatenate([high, rows - high]).astype(low)


def plus_carried(part, other, rows):
    ends = [a[rows:].astype(full) for a in (part, other)]
    count = ends[0].shape[0] // 2
    total = sum(e[:count] + e[count:] for e in ends)
    return jnp.concatenate([plus(part[:rows], other[:rows]), carried(total)])


def inward(part):
    return lax.ppermute(part, "dp", [(0, 1), (3, 2)])


def across(part):
    return lax.ppermute(part, "dp", [(1, 2), (2, 1)])


def outward(part):
    z = lax.axis_index("dp")
    outer = lax.ppermute(part, "dp", [(1, 0), (2, 3)])
    return jnp.where((z == 0) | (z == 3), outer, part)


def ordered(total, other, f):
    return (jnp.where(f == 0, total, other), jnp.where(f == 0, other, total))


def norm_parts(resid):
    center = resid - jnp.mean(resid, axis=-1, keepdims=True)
    rstd = lax.rsqrt(jnp.mean(center * center, axis=-1, keepdims=True) + eps)
    return (center * rstd, rstd)


def norm_backward(scaled, normed, rstd):
    inner = jnp.mean(scaled, axis=-1, keepdims=True)
    along = jnp.mean(scaled * normed, axis=-1, keepdims=True)
    return rstd * (scaled - inner - normed * along)


def gelu_parts(pre):
    cdf = 0.5 * (1.0 + lax.erf(pre * math.sqrt(0.5)))
    slope = cdf + pre * (jnp.exp(-0.5 * pre * pre) * (1.0 / math.sqrt(2.0 * math.pi)))
    return (pre * cdf, slope)


def relative(b):
    return ((b & 1) << 1) | (b >> 1)


def attend_kernel(
    place_in, lens, mask, tokens, wq, wk, wv, wo, bq, bv, compact_out, q_out, k_out, v_out, p_out, ctx_out, near_out, away_out, table_out, count_out
):
    b = pl.program_id(0)
    crop = place_in[0] ^ relative(b)
    length = mask.shape[-1]
    crop_len = lens[crop]
    lane = lax.broadcasted_iota(jnp.int32, (1, length), 1)
    kept = jnp.where(((mask[pl.ds(crop, 1), :] == 1) | (lane == 0)) & (lane < crop_len), 1.0, 0.0)
    rows = lax.broadcasted_iota(jnp.int32, (length, length), 0)
    cols = lax.broadcasted_iota(jnp.int32, (length, length), 1)
    upto = jnp.where(rows <= cols, 1.0, 0.0).astype(low)
    rank = dot(jnp.broadcast_to(kept, (8, length)).astype(low), upto)[0:1]
    place = jnp.where(kept > 0.0, rank - 1.0, -1.0)
    table = jnp.where(place == rows.astype(full), 1.0, 0.0).astype(low)
    count = jnp.sum(kept)

    @pl.when(b == 0)
    def _():
        table_out[...] = table
        count_out[...] = jnp.full(count_out.shape, count, full)

    compact = dot(table, tokens[0]).astype(low)
    compact_out[0] = compact
    query = (dot(compact, wq[...], ((1,), (1,))) + bq[...]).astype(low)
    keys = dot(compact, wk[...], ((1,), (1,))).astype(low)
    values = (dot(compact, wv[...], ((1,), (1,))) + bv[...]).astype(low)
    q_out[0], k_out[0], v_out[0] = query, keys, values
    live = lane.astype(full) < count
    contexts = []
    for h in range(query.shape[1] // HEAD):
        span = slice(h * HEAD, (h + 1) * HEAD)
        scores = dot(query[:, span], keys[:, span], ((1,), (1,))) * (1.0 / math.sqrt(HEAD))
        scores = jnp.where(live, scores, -1e30)
        expo = jnp.exp(scores - jnp.max(scores, axis=1, keepdims=True))
        probs = (expo / jnp.sum(expo, axis=1, keepdims=True)).astype(low)
        p_out[0, h] = probs
        contexts.append(dot(probs, values[:, span]).astype(low))
    context = jnp.concatenate(contexts, axis=1)
    ctx_out[0] = context
    part = dot(context, wo[...]).astype(low)

    @pl.when(b < 2)
    def _():
        near_out[0] = part

    @pl.when(b >= 2)
    def _():
        away_out[0] = part


def attend(tokens, keep_mask, crop_len, place, wq, wk, wv, wo, bq, bv):
    seqs, length, width = tokens.shape
    mine = wq.shape[0]
    heads = mine // HEAD

    def const(*shape):
        return pl.BlockSpec(shape, lambda b, *_: (0,) * len(shape))

    def per(*shape):
        return pl.BlockSpec((1, *shape), lambda b, *_: (b,) + (0,) * len(shape))

    S = jax.ShapeDtypeStruct
    return pl.pallas_call(
        attend_kernel,
        grid_spec=pltpu.PrefetchScalarGridSpec(
            num_scalar_prefetch=2,
            grid=(seqs,),
            in_specs=[
                const(seqs, length),
                pl.BlockSpec((1, length, width), lambda b, place, lens: (place[0] ^ relative(b), 0, 0)),
                const(mine, width),
                const(mine, width),
                const(mine, width),
                const(mine, width),
                const(1, mine),
                const(1, mine),
            ],
            out_specs=[
                per(length, width),
                per(length, mine),
                per(length, mine),
                per(length, mine),
                per(heads, length, length),
                per(length, mine),
                pl.BlockSpec((1, length, width), lambda b, *_: (jnp.minimum(b, 1), 0, 0)),
                pl.BlockSpec((1, length, width), lambda b, *_: (jnp.maximum(b - 2, 0), 0, 0)),
                const(length, length),
                const(8, LANES),
            ],
        ),
        out_shape=[
            S((seqs, length, width), low),
            S((seqs, length, mine), low),
            S((seqs, length, mine), low),
            S((seqs, length, mine), low),
            S((seqs, heads, length, length), low),
            S((seqs, length, mine), low),
            S((2, length, width), low),
            S((2, length, width), low),
            S((length, length), low),
            S((8, LANES), full),
        ],
        name="attend",
    )(place, crop_len, keep_mask, tokens, wq, wk, wv, wo, bq[None], bv[None])


def attend_back_kernel(
    place, g0, g1, g2, g3, compact, q_in, k_in, v_in, p_in, ctx_in, wq, wk, wv, wo, near_out, away_out, *refs
):
    b = pl.program_id(0)
    qk_kept, qk_sent, vo_kept, vo_sent, qb_out, vb_out, grad_s, weights, qb, vb = refs

    @pl.when(b == 0)
    def _():
        weights[...] = jnp.zeros_like(weights)
        qb[...] = jnp.zeros_like(qb)
        vb[...] = jnp.zeros_like(vb)

    for i, g in enumerate((g0, g1, g2, g3)):

        @pl.when(b == i)
        def _(g=g):
            grad_s[...] = g[...]

    scale = 1.0 / math.sqrt(HEAD)
    grad = grad_s[...]
    mine = wq.shape[0]
    query, keys, values = q_in[0], k_in[0], v_in[0]
    context_grad = dot(grad, wo[...], ((1,), (1,))).astype(low)
    query_grads, keys_grads, values_grads = [], [], []
    for h in range(mine // HEAD):
        span = slice(h * HEAD, (h + 1) * HEAD)
        probs = p_in[0, h]
        wide = probs.astype(full)
        probs_grad = dot(context_grad[:, span], values[:, span], ((1,), (1,)))
        inner = jnp.sum(wide * probs_grad, axis=1, keepdims=True)
        score_grad = (wide * (probs_grad - inner)).astype(low)
        query_grads.append((dot(score_grad, keys[:, span]) * scale).astype(low))
        keys_grads.append((dot(score_grad, query[:, span], ((0,), (0,))) * scale).astype(low))
        values_grads.append(dot(probs, context_grad[:, span], ((0,), (0,))).astype(low))
    query_grad = jnp.concatenate(query_grads, axis=1)
    keys_grad = jnp.concatenate(keys_grads, axis=1)
    values_grad = jnp.concatenate(values_grads, axis=1)
    every = jnp.concatenate([query_grad, keys_grad, values_grad], axis=1)
    weights[: 3 * mine] += dot(every, compact[0], ((0,), (0,)))
    weights[3 * mine :] += dot(ctx_in[0], grad, ((0,), (0,)))
    qb[...] += jnp.sum(query_grad.astype(full), axis=0, keepdims=True)
    vb[...] += jnp.sum(values_grad.astype(full), axis=0, keepdims=True)
    back = dot(query_grad, wq[...])
    back += dot(keys_grad, wk[...])
    back += dot(values_grad, wv[...])

    @pl.when(b < 2)
    def _():
        near_out[0] = back.astype(low)

    @pl.when(b >= 2)
    def _():
        away_out[0] = back.astype(low)

    @pl.when(b == pl.num_programs(0) - 1)
    def _():
        f = place[1] >> 1
        for target, block in ((qk_kept, f), (qk_sent, 1 - f), (vo_kept, 2 + f), (vo_sent, 3 - f)):
            target[...] = weights[pl.ds(pl.multiple_of(block * mine, mine), mine), :].astype(low)
        qb_out[...] = qb[...]
        vb_out[...] = vb[...]


def attend_back(place, grads, compact, query, keys, values, probs, context, wq, wk, wv, wo):
    seqs, length, width = compact.shape
    mine = wq.shape[0]
    heads = mine // HEAD

    def const(*shape):
        return pl.BlockSpec(shape, lambda b, *_: (0,) * len(shape))

    def per(*shape):
        return pl.BlockSpec((1, *shape), lambda b, *_: (b,) + (0,) * len(shape))

    S = jax.ShapeDtypeStruct
    return pl.pallas_call(
        attend_back_kernel,
        grid_spec=pltpu.PrefetchScalarGridSpec(
            num_scalar_prefetch=1,
            grid=(seqs,),
            in_specs=[const(length, width)] * 4
            + [
                per(length, width),
                per(length, mine),
                per(length, mine),
                per(length, mine),
                per(heads, length, length),
                per(length, mine),
                const(mine, width),
                const(mine, width),
                const(mine, width),
                const(mine, width),
            ],
            out_specs=[
                pl.BlockSpec((1, length, width), lambda b, *_: (jnp.minimum(b, 1), 0, 0)),
                pl.BlockSpec((1, length, width), lambda b, *_: (jnp.maximum(b - 2, 0), 0, 0)),
                const(mine, width),
                const(mine, width),
                const(mine, width),
                const(mine, width),
                const(1, mine),
                const(1, mine),
            ],
            scratch_shapes=[
                pltpu.VMEM((length, width), low),
                pltpu.VMEM((4 * mine, width), full),
                pltpu.VMEM((1, mine), full),
                pltpu.VMEM((1, mine), full),
            ],
        ),
        out_shape=[S((2, length, width), low)] * 2 + [S((mine, width), low)] * 4 + [S((1, mine), full)] * 2,
        name="attend_back",
    )(place, *grads, compact, query, keys, values, probs, context, wq, wk, wv, wo)


WHOLE, QUARTERS = 4, 6


def gathered_weights(place, wholes, quarters, up, down):
    rows = quarters[1].shape[0] // 2
    shards = [(wholes[0], wholes[1]), (wholes[2], wholes[3])]
    for s in range(2):
        for i, flip, start in ((0, 0, 0), (1, 2, 0), (2, 1, 0), (0, 3, 2)):
            spot = pl.ds(pl.multiple_of((place[1] ^ flip) * rows, rows), rows)
            piece = quarters[3 * s + i]
            up[s, spot, :] = piece[start * rows : (start + 1) * rows]
            down[s, spot, :] = piece[(start + 1) * rows : (start + 2) * rows]
        shards.append((up.at[s], down.at[s]))
    return shards


def ffn_kernel(place, *refs):
    wholes, quarters = refs[:WHOLE], refs[WHOLE : WHOLE + QUARTERS]
    middle, biases, affine, counts = refs[10:14]
    slopes_out, rows_out, output_out, sums_out, pooled_out = refs[14:19]
    up, down = refs[19:]
    shards = gathered_weights(place, wholes, quarters, up, down)
    down_bias, gain, shift = affine[0:1], affine[1:2], affine[2:3]
    length, width = middle.shape
    mid = middle[...]
    mid_low = mid.astype(low)
    total = mid + down_bias
    for s, (up_shard, down_shard) in enumerate(shards):
        hidden, slope = gelu_parts(dot(mid_low, up_shard[...]) + biases[s : s + 1])
        slopes_out[s] = slope.astype(low)
        total += dot(hidden.astype(low), down_shard[...])
    normed, rstd = norm_parts(total)
    output_out[0] = (normed * gain + shift).astype(low)
    count = counts[0:1, 0:1]
    live = jnp.where(lax.broadcasted_iota(jnp.int32, (length, 1), 0).astype(full) < count, 1.0, 0.0)
    factor = rstd * live
    rows_out[:, :width] = normed.astype(low)
    lane = lax.broadcasted_iota(jnp.int32, (length, LANES), 1)
    first = factor.astype(low).astype(full)
    rows_out[:, width:] = jnp.where(lane == 0, first, jnp.where(lane == 1, factor - first, 0.0)).astype(low)
    live_sum = jnp.sum(normed * live, axis=0, keepdims=True)
    sums_out[...] = live_sum
    pooled_out[:, :width] = (live_sum / count * gain + shift).astype(low)
    pooled_out[:, width:] = jnp.broadcast_to(count, (1, LANES)).astype(low)


def ffn_back_kernel(place, *refs):
    wholes, quarters = refs[:WHOLE], refs[WHOLE : WHOLE + QUARTERS]
    slopes, summed, vector, rows, affine = refs[10:15]
    attn_out, one_out, sums_out = refs[15:18]
    up, down = refs[18:]
    shards = gathered_weights(place, wholes, quarters, up, down)
    length, width = one_out.shape
    factor = rows[:, width : width + 1].astype(full) + rows[:, width + 1 : width + 2].astype(full)
    two_grad = norm_backward(jnp.broadcast_to(vector[0:1], (length, width)), rows[:, :width].astype(full), factor)
    ffn_grad = two_grad.astype(low)
    total = two_grad
    for s, (up_shard, down_shard) in enumerate(shards):
        grad = (slopes[s].astype(full) * dot(ffn_grad, down_shard[...], ((1,), (1,)))).astype(low)
        total += dot(grad, up_shard[...], ((1,), (1,)))
    normed, rstd = norm_parts(summed[...])
    one_grad = norm_backward(total * affine[3:4], normed, rstd)
    one_out[...] = one_grad
    attn_grad = one_grad.astype(low)
    attn_out[...] = attn_grad
    sums_out[0:1] = jnp.sum(total * normed, axis=0, keepdims=True)
    sums_out[1:2] = jnp.sum(total, axis=0, keepdims=True)
    sums_out[2:3] = jnp.sum(ffn_grad.astype(full), axis=0, keepdims=True)
    sums_out[3:4] = jnp.sum(attn_grad.astype(full), axis=0, keepdims=True)
    sums_out[4:8] = jnp.zeros((4, width), full)


def with_weights(kernel, name, place, wholes, quarters, operands, outs):
    width, hidden = wholes[0].shape
    inside = pl.BlockSpec(memory_space=pltpu.VMEM)
    return pl.pallas_call(
        kernel,
        in_specs=[pl.BlockSpec(memory_space=pltpu.SMEM)] + [inside] * (WHOLE + QUARTERS + len(operands)),
        out_specs=[inside] * len(outs),
        out_shape=outs,
        scratch_shapes=[pltpu.VMEM((2, width, hidden), low), pltpu.VMEM((2, hidden, width), low)],
        name=name,
    )(place, *wholes, *quarters, *operands)


def ffn_weights_kernel(*refs):
    middles, rows = refs[:8], refs[8:16]
    vectors, up, bias, down = refs[16:20]
    down_out, up_out, bias_out = refs[20:]
    width = middles[0].shape[1]
    down_sum = up_sum = bias_sum = None
    for i in range(8):
        middle = middles[i][...]
        hidden, slope = gelu_parts(dot(middle, up[...]) + bias[...])
        normed = rows[i][:, :width].astype(full)
        factor = rows[i][:, width : width + 1].astype(full) + rows[i][:, width + 1 : width + 2].astype(full)
        vector = vectors[i : i + 1]
        along = jnp.mean(normed * vector, axis=1, keepdims=True)
        ffn_grad = (factor * ((vector - jnp.mean(vector, axis=1, keepdims=True)) - normed * along)).astype(low)
        pre_grad = (slope * dot(ffn_grad, down[...], ((1,), (1,)))).astype(low)
        one = dot(hidden.astype(low), ffn_grad, ((0,), (0,)))
        two = dot(middle, pre_grad, ((0,), (0,)))
        three = jnp.sum(pre_grad.astype(full), axis=0, keepdims=True)
        down_sum, up_sum, bias_sum = (one, two, three) if i == 0 else (down_sum + one, up_sum + two, bias_sum + three)
    down_out[...] = down_sum.astype(low)
    up_out[...] = up_sum.astype(low)
    bias_out[...] = bias_sum


def ffn_weights(middles, rows, vectors, up, bias, down):
    half, width = down.shape
    S = jax.ShapeDtypeStruct
    return pl.pallas_call(
        ffn_weights_kernel,
        out_shape=[S((half, width), low), S((width, half), low), S((1, half), full)],
        name="ffn_weights",
    )(*middles, *rows, vectors, up, bias, down)


def contrast(pooled, key_queue, gathered, halfway, returned):
    width = key_queue.shape[1]
    queries = jnp.concatenate([pooled, swap(pooled, "fsdp", 1)])
    both = queries
    queries = gathered(queries)
    for stride in strides("dp"):
        queries = jnp.concatenate([queries, swap(queries, "dp", stride)])
    queries = halfway(queries)
    logits = dot(queries[:, :width], key_queue, ((1,), (1,))) * inv_temp
    top = jnp.max(logits, axis=1, keepdims=True)
    expo = jnp.exp(logits - top)
    total = jnp.sum(expo, axis=1, keepdims=True)
    rows = dot(expo.astype(low), key_queue)
    state = jnp.concatenate([rows, jnp.broadcast_to(top, (top.shape[0], LANES)), jnp.broadcast_to(total, (top.shape[0], LANES))], axis=1)
    for axis, stride in [("dp", s) for s in reversed(strides("dp"))] + [("fsdp", 1)]:
        half = state.shape[0] // 2
        if axis == "fsdp":
            state = returned(state)
            kept, other = state, swap(jnp.concatenate([state[1:2], state[0:1]]), axis, stride)
        else:
            kept, other = state[:half], swap(state[half:], axis, stride)
        top = jnp.maximum(kept[:, width : width + 1], other[:, width : width + 1])
        summed = kept * jnp.exp(kept[:, width : width + 1] - top) + other * jnp.exp(other[:, width : width + 1] - top)
        state = jnp.concatenate([summed[:, :width], jnp.broadcast_to(top, (top.shape[0], LANES)), summed[:, width + LANES :]], axis=1)
    return (state[:, width : width + 1], state[:, width + LANES : width + LANES + 1], state[:, :width], both)


def per_device(
    tokens,
    keep_mask,
    crop_len,
    pos_index,
    pos_keys,
    key_queue,
    query_weight,
    query_bias,
    key_weight,
    value_weight,
    value_bias,
    out_weight,
    out_bias,
    norm_gain,
    norm_shift,
    up_weight,
    up_bias,
    down_weight,
    down_bias,
    final_gain,
    final_shift,
):
    seqs, length, width = tokens.shape
    hidden = up_weight.shape[1]
    assert seqs == 4 and lax.axis_size("tensor") == 4 and lax.axis_size("fsdp") == 2 and hidden == width
    member = lax.axis_index("tensor")
    f = lax.axis_index("fsdp")
    z = lax.axis_index("dp")
    group = lax.axis_index(("dp", "fsdp"))
    devices = seqs * lax.axis_size("dp") * lax.axis_size("fsdp")
    mine = query_weight.shape[1]
    tie = lax.optimization_barrier
    kind = f * 2 + (z & 1)
    place = jnp.stack([member, kind]).astype(jnp.int32)
    quarter, half = hidden // 4, hidden // 2

    def quarter_of(which):
        return [lax.dynamic_slice_in_dim(w, which * quarter, quarter, 0) for w in (up_weight, down_weight)]

    piece_y = swap(jnp.concatenate(quarter_of(kind) + quarter_of(kind ^ 3)), "tensor", 2)
    wholes = [up_weight, down_weight, swap(up_weight, "tensor", 1), swap(down_weight, "tensor", 1)]
    up_half = lax.dynamic_slice_in_dim(up_weight, f * half, half, 1)
    down_half = lax.dynamic_slice_in_dim(down_weight, f * half, half, 0)
    bias_half = lax.dynamic_slice_in_dim(up_bias[None], f * half, half, 1)

    known = jnp.concatenate([pos_keys, swap(pos_keys, "fsdp", 1)])
    compact, query, keys, values, probs, context, near, away, table, counts = attend(
        tokens, keep_mask, crop_len, place, query_weight.T, key_weight.T, value_weight.T, out_weight, query_bias, value_bias
    )
    affine = jnp.stack([down_bias, final_gain, final_shift, norm_gain])
    for stride in strides("dp"):
        known = jnp.concatenate([known, swap(known, "dp", stride)])
    compact, piece_y, known, wholes, affine, up_half, down_half, bias_half = tie(
        (compact, piece_y, known, wholes, affine, up_half, down_half, bias_half)
    )
    other = swap(away, "tensor", 1)
    share = pos_keys.shape[0]
    spot = jnp.arange(devices, dtype=jnp.int32)[None]
    mates = jnp.stack([group, group ^ 1]) * share + member
    wanted = jnp.sum(jnp.where(spot == mates[:, None], pos_index[None], 0), axis=1, keepdims=True)
    chosen = jnp.where(((spot // share) ^ group) * share + spot % share == wanted, 1.0, 0.0).astype(low)
    sent, piece_y = tie((plus(near[1], other[1]), piece_y))
    first = piece_y[: 2 * quarter]
    piece_x = swap(first, "fsdp", 1)
    piece_z = swap(first, "dp", 1)
    attn_out = near[0].astype(full) + other[0].astype(full) + swap(sent, "tensor", 2).astype(full)
    attn_out, bias_own = tie((attn_out, up_bias))
    bias_far = swap(bias_own[None], "tensor", 2)
    bias_pair = jnp.concatenate([up_bias[None], bias_far])
    bias_pair = jnp.concatenate([bias_pair, swap(bias_pair, "tensor", 1)])
    biases = jnp.stack([bias_pair[0], bias_pair[2], bias_pair[1], bias_pair[3]])
    quarters = [piece_y, piece_x, piece_z]
    quarters = quarters + [swap(p, "tensor", 1) for p in quarters]

    summed = compact[0].astype(full) + attn_out + out_bias
    middle = norm_parts(summed)[0] * norm_gain + norm_shift
    middle_low = middle.astype(low)
    quarters, biases, chosen, middle, middle_low = tie((quarters, biases, chosen, middle, middle_low))
    S = jax.ShapeDtypeStruct
    slopes, rows, output, live_sum, pooled = with_weights(
        ffn_kernel,
        "ffn",
        place,
        wholes,
        quarters,
        [middle, biases, affine, counts],
        [
            S((4, length, hidden), low),
            S((length, width + LANES), low),
            S((1, length, width), low),
            S((1, width), full),
            S((1, width + LANES), low),
        ],
    )

    middle_x, middle_y = swap(middle_low, "fsdp", 1), swap(middle_low, "tensor", 2)
    pooled, middle_x, middle_y = tie((pooled, middle_x, middle_y))
    pairs = {}

    def gathered(queries):
        queries, row_own, mid = tie((queries, rows, middle_x))
        pairs["x"], pairs["y"] = swap(row_own, "fsdp", 1), swap(row_own, "tensor", 2)
        pairs["mid"] = swap(mid, "tensor", 2)
        return queries

    def halfway(queries):
        queries, pairs["mid"] = tie((queries, pairs["mid"]))
        return queries

    def returned(state):
        state, pairs["x"], pairs["y"] = tie((state, pairs["x"], pairs["y"]))
        return state

    positive = dot(chosen, known)
    top, total, key_sum, pooled_pair = contrast(pooled, key_queue, gathered, halfway, returned)
    count_pair = pooled_pair[:, width : width + 1].astype(full)
    middle_pair = [middle_low, middle_x, middle_y, pairs["mid"]]
    rows_pair = [rows, pairs["x"], pairs["y"]]
    middles = middle_pair + [swap(p, "tensor", 1) for p in middle_pair]
    rows_core = [swap(p, "tensor", 1) for p in rows_pair]

    pos_logit = jnp.sum(pooled_pair[:, :width].astype(full) * positive, axis=1, keepdims=True) * inv_temp
    top_final = jnp.maximum(top, pos_logit)
    lse = top_final + jnp.log(total * jnp.exp(top - top_final) + jnp.exp(pos_logit - top_final))
    loss_part = jnp.broadcast_to((lse - pos_logit) / devices, (2, width))
    step = loss_scale * inv_temp
    pooled_grad = key_sum * (step * jnp.exp(top - lse)) + step * (jnp.exp(pos_logit - lse) - 1.0) * positive
    result_row = pooled_grad / count_pair
    vector_pair = result_row * final_gain
    final_gain_part = result_row[0:1] * live_sum

    vector_pair, rows_core = tie((vector_pair, rows_core))
    attn_grad, one_grad, sums = with_weights(
        ffn_back_kernel,
        "ffn_back",
        place,
        wholes,
        quarters,
        [slopes, summed, vector_pair, rows, affine],
        [S((length, width), low), S((length, width), full), S((8, width), full)],
    )
    vectors_far, rows_far, attn_grad, middles, sums = tie((swap(vector_pair, "tensor", 2), swap(pairs["x"], "tensor", 2), attn_grad, middles, sums))
    vectors_far = jnp.concatenate([vector_pair, vectors_far])
    vectors_all = jnp.concatenate([vectors_far, swap(vectors_far, "tensor", 1)])
    rows_all = rows_pair + [rows_far] + rows_core + [swap(rows_far, "tensor", 1)]
    vectors = jnp.concatenate([final_gain_part, pooled_grad[0:1], sums[0:4], loss_part[0:1]])
    down, up, up_bias_half = ffn_weights(middles, rows_all, vectors_all, up_half, bias_half, down_half)
    vectors = vectors + swap(vectors, "tensor", 1)
    attn_far, attn_core, down, up, vectors = tie((swap(attn_grad, "tensor", 2), swap(attn_grad, "tensor", 1), down, up, vectors))
    attn_grads = [attn_grad, attn_far, attn_core, swap(attn_far, "tensor", 1)]

    near_in, away_in, qk_kept, qk_sent, vo_kept, vo_sent, query_bias_part, value_bias_part = attend_back(
        place, attn_grads, compact, query, keys, values, probs, context, query_weight.T, key_weight.T, value_weight.T, out_weight
    )
    line = lax.axis_size("dp") == 4
    moved = inward(down) if line else down
    qk_sent, vo_sent, near_in, away_in, moved, vectors = tie((qk_sent, vo_sent, near_in, away_in, moved, vectors))
    vectors = vectors + swap(vectors, "tensor", 2)
    pad = jnp.zeros((1, width - 2 * mine), full)
    narrow = jnp.concatenate([query_bias_part, value_bias_part, pad], axis=1)
    blank = jnp.zeros_like(up_bias_half)
    up_bias_part = jnp.concatenate([jnp.where(f == 0, up_bias_half, blank), jnp.where(f == 0, blank, up_bias_half)], axis=1)
    vectors = jnp.concatenate([vectors, narrow, up_bias_part, jnp.zeros((7, width), full)])
    extra = carried(vectors)
    if line:
        up_in = inward(up)
        qk = plus(qk_kept, swap(qk_sent, "fsdp", 1))
        vo = plus_carried(jnp.concatenate([vo_kept, extra]), swap(jnp.concatenate([vo_sent, extra]), "fsdp", 1), mine)
        down = plus(down, moved)
        down = plus(down, across(down))
        qk, up_in = tie((qk, up_in))
        up = plus(up, up_in)
        vo, down = tie((vo, down))
        qk = plus(qk, inward(qk))
        vo = plus_carried(vo, inward(vo), mine)
        up = plus(up, across(up))
        up, vo = tie((up, vo))
        qk = plus(qk, across(qk))
        down = outward(down)
        vo = plus_carried(vo, across(vo), mine)
        up = outward(up)
        qk = outward(qk)
        vo = outward(vo)
        extra, vo = vo[mine:].astype(full), vo[:mine]
        vectors = extra[:16] + extra[16:]
    else:
        down, up, qk, vo = [
            lax.psum(a.astype(full), "dp").astype(low)
            for a in (down, up, plus(qk_kept, swap(qk_sent, "fsdp", 1)), plus(vo_kept, swap(vo_sent, "fsdp", 1)))
        ]
        vectors = lax.psum(vectors + swap(vectors, "fsdp", 1), "dp")
    down_other, up_other, qk_other, vo_other = [swap(a, "fsdp", 1) for a in (down, up, qk, vo)]
    down_weight_grad = jnp.concatenate(ordered(down, down_other, f)).astype(full)
    up_weight_grad = jnp.concatenate(ordered(up, up_other, f), axis=1).astype(full)
    query_grad, key_grad = ordered(qk, qk_other, f)
    value_grad, out_grad = ordered(vo, vo_other, f)

    other_in = swap(away_in, "tensor", 1)
    far_in = swap(plus(near_in[1], other_in[1]), "tensor", 2)
    back = near_in[0].astype(full) + other_in[0].astype(full) + far_in.astype(full)
    compact_grad = (one_grad + back).astype(low)
    input_grad = dot(table, compact_grad, ((0,), (0,))).astype(low)
    return (
        output,
        input_grad[None],
        query_grad.T.astype(full),
        vectors[7, :mine],
        key_grad.T.astype(full),
        value_grad.T.astype(full),
        vectors[7, mine : 2 * mine],
        out_grad.astype(full),
        vectors[5],
        vectors[2],
        vectors[3],
        up_weight_grad,
        vectors[8],
        down_weight_grad,
        vectors[4],
        vectors[0],
        vectors[1],
        vectors[6, 0],
    )


def solution(mesh):
    placed = (
        P(("dp", "fsdp"), None, None),
        P(("dp", "fsdp"), None),
        P(("dp", "fsdp")),
        P(),
        P(("dp", "fsdp"), None),
        P(("dp", "fsdp"), None),
        P(None, "tensor"),
        P("tensor"),
        P(None, "tensor"),
        P(None, "tensor"),
        P("tensor"),
        P("tensor", None),
        P(),
        P(),
        P(),
        P(None, "tensor"),
        P("tensor"),
        P("tensor", None),
        P(),
        P(),
        P(),
    )
    return jax.shard_map(
        per_device,
        mesh=mesh,
        in_specs=placed,
        out_specs=(
            P(("dp", "fsdp", "tensor"), None, None),
            P(("dp", "fsdp", "tensor"), None, None),
            P(None, "tensor"),
            P("tensor"),
            P(None, "tensor"),
            P(None, "tensor"),
            P("tensor"),
            P("tensor", None),
            P(),
            P(),
            P(),
            P(None, "tensor"),
            P("tensor"),
            P("tensor", None),
            P(),
            P(),
            P(),
            P(),
        ),
        check_vma=False,
    )
```

```python
import math

import jax
import jax.numpy as jnp
from jax import lax
from jax.experimental import pallas as pl
from jax.experimental.pallas import tpu as pltpu
from jax.sharding import PartitionSpec as P

HEAD = 64
eps = 1e-12
inv_temp = 20.0
loss_scale = 256.0
low = jnp.bfloat16
full = jnp.float32
LANES = 128


def dot(a, b, dims=((1,), (0,))):
    return lax.dot_general(a, b, (dims, ((), ())), preferred_element_type=full)


def swap(array, axis, stride):
    size = lax.axis_size(axis)
    return lax.ppermute(array, axis, [(i, i ^ stride) for i in range(size)])


def strides(axis):
    size = lax.axis_size(axis)
    assert size & (size - 1) == 0
    return [1 << k for k in range(size.bit_length() - 1)]


def plus(part, other):
    return (part.astype(full) + other.astype(full)).astype(low)


def carried(rows):
    high = lax.reduce_precision(rows, 8, 7)
    return jnp.concatenate([high, rows - high]).astype(low)


def plus_carried(part, other, rows):
    ends = [a[rows:].astype(full) for a in (part, other)]
    count = ends[0].shape[0] // 2
    total = sum(e[:count] + e[count:] for e in ends)
    return jnp.concatenate([plus(part[:rows], other[:rows]), carried(total)])


def inward(part):
    return lax.ppermute(part, "dp", [(0, 1), (3, 2)])


def across(part):
    return lax.ppermute(part, "dp", [(1, 2), (2, 1)])


def outward(part):
    z = lax.axis_index("dp")
    outer = lax.ppermute(part, "dp", [(1, 0), (2, 3)])
    return jnp.where((z == 0) | (z == 3), outer, part)


def ordered(total, other, f):
    return (jnp.where(f == 0, total, other), jnp.where(f == 0, other, total))


def norm_parts(resid):
    center = resid - jnp.mean(resid, axis=-1, keepdims=True)
    rstd = lax.rsqrt(jnp.mean(center * center, axis=-1, keepdims=True) + eps)
    return (center * rstd, rstd)


def norm_backward(scaled, normed, rstd):
    inner = jnp.mean(scaled, axis=-1, keepdims=True)
    along = jnp.mean(scaled * normed, axis=-1, keepdims=True)
    return rstd * (scaled - inner - normed * along)


def gelu_parts(pre):
    cdf = 0.5 * (1.0 + lax.erf(pre * math.sqrt(0.5)))
    slope = cdf + pre * (jnp.exp(-0.5 * pre * pre) * (1.0 / math.sqrt(2.0 * math.pi)))
    return (pre * cdf, slope)


def relative(b):
    return ((b & 1) << 1) | (b >> 1)


def attend_kernel(
    place_in, lens, mask, tokens, wq, wk, wv, wo, bq, bv, compact_out, q_out, k_out, v_out, p_out, ctx_out, near_out, away_out, table_out, count_out
):
    b = pl.program_id(0)
    crop = place_in[0] ^ relative(b)
    length = mask.shape[-1]
    crop_len = lens[crop]
    lane = lax.broadcasted_iota(jnp.int32, (1, length), 1)
    kept = jnp.where(((mask[pl.ds(crop, 1), :] == 1) | (lane == 0)) & (lane < crop_len), 1.0, 0.0)
    rows = lax.broadcasted_iota(jnp.int32, (length, length), 0)
    cols = lax.broadcasted_iota(jnp.int32, (length, length), 1)
    upto = jnp.where(rows <= cols, 1.0, 0.0).astype(low)
    rank = dot(jnp.broadcast_to(kept, (8, length)).astype(low), upto)[0:1]
    place = jnp.where(kept > 0.0, rank - 1.0, -1.0)
    table = jnp.where(place == rows.astype(full), 1.0, 0.0).astype(low)
    count = jnp.sum(kept)

    @pl.when(b == 0)
    def _():
        table_out[...] = table
        count_out[...] = jnp.full(count_out.shape, count, full)

    compact = dot(table, tokens[0]).astype(low)
    compact_out[0] = compact
    query = (dot(compact, wq[...], ((1,), (1,))) + bq[...]).astype(low)
    keys = dot(compact, wk[...], ((1,), (1,))).astype(low)
    values = (dot(compact, wv[...], ((1,), (1,))) + bv[...]).astype(low)
    q_out[0], k_out[0], v_out[0] = query, keys, values
    live = lane.astype(full) < count
    contexts = []
    for h in range(query.shape[1] // HEAD):
        span = slice(h * HEAD, (h + 1) * HEAD)
        scores = dot(query[:, span], keys[:, span], ((1,), (1,))) * (1.0 / math.sqrt(HEAD))
        scores = jnp.where(live, scores, -1e30)
        expo = jnp.exp(scores - jnp.max(scores, axis=1, keepdims=True))
        probs = (expo / jnp.sum(expo, axis=1, keepdims=True)).astype(low)
        p_out[0, h] = probs
        contexts.append(dot(probs, values[:, span]).astype(low))
    context = jnp.concatenate(contexts, axis=1)
    ctx_out[0] = context
    part = dot(context, wo[...]).astype(low)

    @pl.when(b < 2)
    def _():
        near_out[0] = part

    @pl.when(b >= 2)
    def _():
        away_out[0] = part


def attend(tokens, keep_mask, crop_len, place, wq, wk, wv, wo, bq, bv):
    seqs, length, width = tokens.shape
    mine = wq.shape[0]
    heads = mine // HEAD

    def const(*shape):
        return pl.BlockSpec(shape, lambda b, *_: (0,) * len(shape))

    def per(*shape):
        return pl.BlockSpec((1, *shape), lambda b, *_: (b,) + (0,) * len(shape))

    S = jax.ShapeDtypeStruct
    return pl.pallas_call(
        attend_kernel,
        grid_spec=pltpu.PrefetchScalarGridSpec(
            num_scalar_prefetch=2,
            grid=(seqs,),
            in_specs=[
                const(seqs, length),
                pl.BlockSpec((1, length, width), lambda b, place, lens: (place[0] ^ relative(b), 0, 0)),
                const(mine, width),
                const(mine, width),
                const(mine, width),
                const(mine, width),
                const(1, mine),
                const(1, mine),
            ],
            out_specs=[
                per(length, width),
                per(length, mine),
                per(length, mine),
                per(length, mine),
                per(heads, length, length),
                per(length, mine),
                pl.BlockSpec((1, length, width), lambda b, *_: (jnp.minimum(b, 1), 0, 0)),
                pl.BlockSpec((1, length, width), lambda b, *_: (jnp.maximum(b - 2, 0), 0, 0)),
                const(length, length),
                const(8, LANES),
            ],
        ),
        out_shape=[
            S((seqs, length, width), low),
            S((seqs, length, mine), low),
            S((seqs, length, mine), low),
            S((seqs, length, mine), low),
            S((seqs, heads, length, length), low),
            S((seqs, length, mine), low),
            S((2, length, width), low),
            S((2, length, width), low),
            S((length, length), low),
            S((8, LANES), full),
        ],
        name="attend",
    )(place, crop_len, keep_mask, tokens, wq, wk, wv, wo, bq[None], bv[None])


def attend_back_kernel(
    place, g0, g1, g2, g3, compact, q_in, k_in, v_in, p_in, ctx_in, wq, wk, wv, wo, near_out, away_out, *refs
):
    b = pl.program_id(0)
    qk_kept, qk_sent, vo_kept, vo_sent, qb_out, vb_out, grad_s, weights, qb, vb = refs

    @pl.when(b == 0)
    def _():
        weights[...] = jnp.zeros_like(weights)
        qb[...] = jnp.zeros_like(qb)
        vb[...] = jnp.zeros_like(vb)

    for i, g in enumerate((g0, g1, g2, g3)):

        @pl.when(b == i)
        def _(g=g):
            grad_s[...] = g[...]

    scale = 1.0 / math.sqrt(HEAD)
    grad = grad_s[...]
    mine = wq.shape[0]
    query, keys, values = q_in[0], k_in[0], v_in[0]
    context_grad = dot(grad, wo[...], ((1,), (1,))).astype(low)
    query_grads, keys_grads, values_grads = [], [], []
    for h in range(mine // HEAD):
        span = slice(h * HEAD, (h + 1) * HEAD)
        probs = p_in[0, h]
        wide = probs.astype(full)
        probs_grad = dot(context_grad[:, span], values[:, span], ((1,), (1,)))
        inner = jnp.sum(wide * probs_grad, axis=1, keepdims=True)
        score_grad = (wide * (probs_grad - inner)).astype(low)
        query_grads.append((dot(score_grad, keys[:, span]) * scale).astype(low))
        keys_grads.append((dot(score_grad, query[:, span], ((0,), (0,))) * scale).astype(low))
        values_grads.append(dot(probs, context_grad[:, span], ((0,), (0,))).astype(low))
    query_grad = jnp.concatenate(query_grads, axis=1)
    keys_grad = jnp.concatenate(keys_grads, axis=1)
    values_grad = jnp.concatenate(values_grads, axis=1)
    every = jnp.concatenate([query_grad, keys_grad, values_grad], axis=1)
    weights[: 3 * mine] += dot(every, compact[0], ((0,), (0,)))
    weights[3 * mine :] += dot(ctx_in[0], grad, ((0,), (0,)))
    qb[...] += jnp.sum(query_grad.astype(full), axis=0, keepdims=True)
    vb[...] += jnp.sum(values_grad.astype(full), axis=0, keepdims=True)
    back = dot(query_grad, wq[...])
    back += dot(keys_grad, wk[...])
    back += dot(values_grad, wv[...])

    @pl.when(b < 2)
    def _():
        near_out[0] = back.astype(low)

    @pl.when(b >= 2)
    def _():
        away_out[0] = back.astype(low)

    @pl.when(b == pl.num_programs(0) - 1)
    def _():
        f = place[1] >> 1
        for target, block in ((qk_kept, f), (qk_sent, 1 - f), (vo_kept, 2 + f), (vo_sent, 3 - f)):
            target[...] = weights[pl.ds(pl.multiple_of(block * mine, mine), mine), :].astype(low)
        qb_out[...] = qb[...]
        vb_out[...] = vb[...]


def attend_back(place, grads, compact, query, keys, values, probs, context, wq, wk, wv, wo):
    seqs, length, width = compact.shape
    mine = wq.shape[0]
    heads = mine // HEAD

    def const(*shape):
        return pl.BlockSpec(shape, lambda b, *_: (0,) * len(shape))

    def per(*shape):
        return pl.BlockSpec((1, *shape), lambda b, *_: (b,) + (0,) * len(shape))

    S = jax.ShapeDtypeStruct
    return pl.pallas_call(
        attend_back_kernel,
        grid_spec=pltpu.PrefetchScalarGridSpec(
            num_scalar_prefetch=1,
            grid=(seqs,),
            in_specs=[const(length, width)] * 4
            + [
                per(length, width),
                per(length, mine),
                per(length, mine),
                per(length, mine),
                per(heads, length, length),
                per(length, mine),
                const(mine, width),
                const(mine, width),
                const(mine, width),
                const(mine, width),
            ],
            out_specs=[
                pl.BlockSpec((1, length, width), lambda b, *_: (jnp.minimum(b, 1), 0, 0)),
                pl.BlockSpec((1, length, width), lambda b, *_: (jnp.maximum(b - 2, 0), 0, 0)),
                const(mine, width),
                const(mine, width),
                const(mine, width),
                const(mine, width),
                const(1, mine),
                const(1, mine),
            ],
            scratch_shapes=[
                pltpu.VMEM((length, width), low),
                pltpu.VMEM((4 * mine, width), full),
                pltpu.VMEM((1, mine), full),
                pltpu.VMEM((1, mine), full),
            ],
        ),
        out_shape=[S((2, length, width), low)] * 2 + [S((mine, width), low)] * 4 + [S((1, mine), full)] * 2,
        name="attend_back",
    )(place, *grads, compact, query, keys, values, probs, context, wq, wk, wv, wo)


WHOLE, QUARTERS = 4, 6


def gathered_weights(place, wholes, quarters, up, down):
    rows = quarters[1].shape[0] // 2
    shards = [(wholes[0], wholes[1]), (wholes[2], wholes[3])]
    for s in range(2):
        for i, flip, start in ((0, 0, 0), (1, 2, 0), (2, 1, 0), (0, 3, 2)):
            spot = pl.ds(pl.multiple_of((place[1] ^ flip) * rows, rows), rows)
            piece = quarters[3 * s + i]
            up[s, spot, :] = piece[start * rows : (start + 1) * rows]
            down[s, spot, :] = piece[(start + 1) * rows : (start + 2) * rows]
        shards.append((up.at[s], down.at[s]))
    return shards


def ffn_kernel(place, *refs):
    wholes, quarters = refs[:WHOLE], refs[WHOLE : WHOLE + QUARTERS]
    middle, biases, affine, counts = refs[10:14]
    slopes_out, rows_out, output_out, sums_out, pooled_out = refs[14:19]
    up, down = refs[19:]
    shards = gathered_weights(place, wholes, quarters, up, down)
    down_bias, gain, shift = affine[0:1], affine[1:2], affine[2:3]
    length, width = middle.shape
    mid = middle[...]
    mid_low = mid.astype(low)
    total = mid + down_bias
    for s, (up_shard, down_shard) in enumerate(shards):
        hidden, slope = gelu_parts(dot(mid_low, up_shard[...]) + biases[s : s + 1])
        slopes_out[s] = slope.astype(low)
        total += dot(hidden.astype(low), down_shard[...])
    normed, rstd = norm_parts(total)
    output_out[0] = (normed * gain + shift).astype(low)
    count = counts[0:1, 0:1]
    live = jnp.where(lax.broadcasted_iota(jnp.int32, (length, 1), 0).astype(full) < count, 1.0, 0.0)
    factor = rstd * live
    rows_out[:, :width] = normed.astype(low)
    lane = lax.broadcasted_iota(jnp.int32, (length, LANES), 1)
    first = factor.astype(low).astype(full)
    rows_out[:, width:] = jnp.where(lane == 0, first, jnp.where(lane == 1, factor - first, 0.0)).astype(low)
    live_sum = jnp.sum(normed * live, axis=0, keepdims=True)
    sums_out[...] = live_sum
    pooled_out[:, :width] = (live_sum / count * gain + shift).astype(low)
    pooled_out[:, width:] = jnp.broadcast_to(count, (1, LANES)).astype(low)


def ffn_back_kernel(place, *refs):
    wholes, quarters = refs[:WHOLE], refs[WHOLE : WHOLE + QUARTERS]
    slopes, summed, vector, rows, affine = refs[10:15]
    attn_out, one_out, sums_out = refs[15:18]
    up, down = refs[18:]
    shards = gathered_weights(place, wholes, quarters, up, down)
    length, width = one_out.shape
    factor = rows[:, width : width + 1].astype(full) + rows[:, width + 1 : width + 2].astype(full)
    two_grad = norm_backward(jnp.broadcast_to(vector[0:1], (length, width)), rows[:, :width].astype(full), factor)
    ffn_grad = two_grad.astype(low)
    total = two_grad
    for s, (up_shard, down_shard) in enumerate(shards):
        grad = (slopes[s].astype(full) * dot(ffn_grad, down_shard[...], ((1,), (1,)))).astype(low)
        total += dot(grad, up_shard[...], ((1,), (1,)))
    normed, rstd = norm_parts(summed[...])
    one_grad = norm_backward(total * affine[3:4], normed, rstd)
    one_out[...] = one_grad
    attn_grad = one_grad.astype(low)
    attn_out[...] = attn_grad
    sums_out[0:1] = jnp.sum(total * normed, axis=0, keepdims=True)
    sums_out[1:2] = jnp.sum(total, axis=0, keepdims=True)
    sums_out[2:3] = jnp.sum(ffn_grad.astype(full), axis=0, keepdims=True)
    sums_out[3:4] = jnp.sum(attn_grad.astype(full), axis=0, keepdims=True)
    sums_out[4:8] = jnp.zeros((4, width), full)


def with_weights(kernel, name, place, wholes, quarters, operands, outs):
    width, hidden = wholes[0].shape
    inside = pl.BlockSpec(memory_space=pltpu.VMEM)
    return pl.pallas_call(
        kernel,
        in_specs=[pl.BlockSpec(memory_space=pltpu.SMEM)] + [inside] * (WHOLE + QUARTERS + len(operands)),
        out_specs=[inside] * len(outs),
        out_shape=outs,
        scratch_shapes=[pltpu.VMEM((2, width, hidden), low), pltpu.VMEM((2, hidden, width), low)],
        name=name,
    )(place, *wholes, *quarters, *operands)


def ffn_weights_kernel(*refs):
    middles, rows = refs[:8], refs[8:16]
    vectors, (up, bias, down) = refs[16:20], refs[20:23]
    down_out, up_out, bias_out = refs[23:]
    width = middles[0].shape[1]
    down_sum = up_sum = bias_sum = None
    for i in range(8):
        middle = middles[i][...]
        hidden, slope = gelu_parts(dot(middle, up[...]) + bias[...])
        normed = rows[i][:, :width].astype(full)
        factor = rows[i][:, width : width + 1].astype(full) + rows[i][:, width + 1 : width + 2].astype(full)
        vector = vectors[i // 2][i % 2 : i % 2 + 1]
        along = jnp.mean(normed * vector, axis=1, keepdims=True)
        ffn_grad = (factor * ((vector - jnp.mean(vector, axis=1, keepdims=True)) - normed * along)).astype(low)
        pre_grad = (slope * dot(ffn_grad, down[...], ((1,), (1,)))).astype(low)
        one = dot(hidden.astype(low), ffn_grad, ((0,), (0,)))
        two = dot(middle, pre_grad, ((0,), (0,)))
        three = jnp.sum(pre_grad.astype(full), axis=0, keepdims=True)
        down_sum, up_sum, bias_sum = (one, two, three) if i == 0 else (down_sum + one, up_sum + two, bias_sum + three)
    down_out[...] = down_sum.astype(low)
    up_out[...] = up_sum.astype(low)
    bias_out[...] = bias_sum


def ffn_weights(middles, rows, vectors, up, bias, down):
    half, width = down.shape
    S = jax.ShapeDtypeStruct
    return pl.pallas_call(
        ffn_weights_kernel,
        out_shape=[S((half, width), low), S((width, half), low), S((1, half), full)],
        name="ffn_weights",
    )(*middles, *rows, *vectors, up, bias, down)


def contrast(pooled, key_queue, gathered, halfway, returned):
    width = key_queue.shape[1]
    queries = jnp.concatenate([pooled, swap(pooled, "fsdp", 1)])
    both = queries
    queries = gathered(queries)
    for stride in strides("dp"):
        queries = jnp.concatenate([queries, swap(queries, "dp", stride)])
    queries = halfway(queries)
    logits = dot(queries[:, :width], key_queue, ((1,), (1,))) * inv_temp
    top = jnp.max(logits, axis=1, keepdims=True)
    expo = jnp.exp(logits - top)
    total = jnp.sum(expo, axis=1, keepdims=True)
    rows = dot(expo.astype(low), key_queue)
    state = jnp.concatenate([rows, jnp.broadcast_to(top, (top.shape[0], LANES)), jnp.broadcast_to(total, (top.shape[0], LANES))], axis=1)
    for axis, stride in [("dp", s) for s in reversed(strides("dp"))] + [("fsdp", 1)]:
        half = state.shape[0] // 2
        if axis == "fsdp":
            state = returned(state)
            kept, other = state, swap(jnp.concatenate([state[1:2], state[0:1]]), axis, stride)
        else:
            kept, other = state[:half], swap(state[half:], axis, stride)
        top = jnp.maximum(kept[:, width : width + 1], other[:, width : width + 1])
        summed = kept * jnp.exp(kept[:, width : width + 1] - top) + other * jnp.exp(other[:, width : width + 1] - top)
        state = jnp.concatenate([summed[:, :width], jnp.broadcast_to(top, (top.shape[0], LANES)), summed[:, width + LANES :]], axis=1)
    return (state[:, width : width + 1], state[:, width + LANES : width + LANES + 1], state[:, :width], both)


def per_device(
    tokens,
    keep_mask,
    crop_len,
    pos_index,
    pos_keys,
    key_queue,
    query_weight,
    query_bias,
    key_weight,
    value_weight,
    value_bias,
    out_weight,
    out_bias,
    norm_gain,
    norm_shift,
    up_weight,
    up_bias,
    down_weight,
    down_bias,
    final_gain,
    final_shift,
):
    seqs, length, width = tokens.shape
    hidden = up_weight.shape[1]
    assert seqs == 4 and lax.axis_size("tensor") == 4 and lax.axis_size("fsdp") == 2 and hidden == width
    member = lax.axis_index("tensor")
    f = lax.axis_index("fsdp")
    z = lax.axis_index("dp")
    group = lax.axis_index(("dp", "fsdp"))
    devices = seqs * lax.axis_size("dp") * lax.axis_size("fsdp")
    mine = query_weight.shape[1]
    tie = lax.optimization_barrier
    kind = f * 2 + (z & 1)
    place = jnp.stack([member, kind]).astype(jnp.int32)
    quarter, half = hidden // 4, hidden // 2

    def quarter_of(which):
        return [lax.dynamic_slice_in_dim(w, which * quarter, quarter, 0) for w in (up_weight, down_weight)]

    piece_y = swap(jnp.concatenate(quarter_of(kind) + quarter_of(kind ^ 3)), "tensor", 2)
    wholes = [up_weight, down_weight, swap(up_weight, "tensor", 1), swap(down_weight, "tensor", 1)]
    up_half = lax.dynamic_slice_in_dim(up_weight, f * half, half, 1)
    down_half = lax.dynamic_slice_in_dim(down_weight, f * half, half, 0)
    bias_half = lax.dynamic_slice_in_dim(up_bias[None], f * half, half, 1)

    known = jnp.concatenate([pos_keys, swap(pos_keys, "fsdp", 1)])
    compact, query, keys, values, probs, context, near, away, table, counts = attend(
        tokens, keep_mask, crop_len, place, query_weight.T, key_weight.T, value_weight.T, out_weight, query_bias, value_bias
    )
    affine = jnp.stack([down_bias, final_gain, final_shift, norm_gain])
    for stride in strides("dp"):
        known = jnp.concatenate([known, swap(known, "dp", stride)])
    compact, piece_y, known, wholes, affine, up_half, down_half, bias_half = tie(
        (compact, piece_y, known, wholes, affine, up_half, down_half, bias_half)
    )
    other = swap(away, "tensor", 1)
    share = pos_keys.shape[0]
    spot = jnp.arange(devices, dtype=jnp.int32)[None]
    mates = jnp.stack([group, group ^ 1]) * share + member
    wanted = jnp.sum(jnp.where(spot == mates[:, None], pos_index[None], 0), axis=1, keepdims=True)
    chosen = jnp.where(((spot // share) ^ group) * share + spot % share == wanted, 1.0, 0.0).astype(low)
    sent, piece_y = tie((plus(near[1], other[1]), piece_y))
    first = piece_y[: 2 * quarter]
    piece_x = swap(first, "fsdp", 1)
    piece_z = swap(first, "dp", 1)
    attn_out = near[0].astype(full) + other[0].astype(full) + swap(sent, "tensor", 2).astype(full)
    attn_out, bias_own = tie((attn_out, up_bias))
    bias_far = swap(bias_own[None], "tensor", 2)
    bias_pair = jnp.concatenate([up_bias[None], bias_far])
    bias_pair = jnp.concatenate([bias_pair, swap(bias_pair, "tensor", 1)])
    biases = jnp.stack([bias_pair[0], bias_pair[2], bias_pair[1], bias_pair[3]])
    quarters = [piece_y, piece_x, piece_z]
    quarters = quarters + [swap(p, "tensor", 1) for p in quarters]

    summed = compact[0].astype(full) + attn_out + out_bias
    middle = norm_parts(summed)[0] * norm_gain + norm_shift
    middle_low = middle.astype(low)
    quarters, biases, chosen, middle, middle_low = tie((quarters, biases, chosen, middle, middle_low))
    S = jax.ShapeDtypeStruct
    slopes, rows, output, live_sum, pooled = with_weights(
        ffn_kernel,
        "ffn",
        place,
        wholes,
        quarters,
        [middle, biases, affine, counts],
        [
            S((4, length, hidden), low),
            S((length, width + LANES), low),
            S((1, length, width), low),
            S((1, width), full),
            S((1, width + LANES), low),
        ],
    )

    middle_x, middle_y = swap(middle_low, "fsdp", 1), swap(middle_low, "tensor", 2)
    pooled, middle_x, middle_y = tie((pooled, middle_x, middle_y))
    pairs = {}

    def gathered(queries):
        queries, row_own, mid = tie((queries, rows, middle_x))
        pairs["x"], pairs["y"] = swap(row_own, "fsdp", 1), swap(row_own, "tensor", 2)
        pairs["mid"] = swap(mid, "tensor", 2)
        return queries

    def halfway(queries):
        queries, pairs["mid"] = tie((queries, pairs["mid"]))
        return queries

    def returned(state):
        state, pairs["x"], pairs["y"] = tie((state, pairs["x"], pairs["y"]))
        return state

    positive = dot(chosen, known)
    top, total, key_sum, pooled_pair = contrast(pooled, key_queue, gathered, halfway, returned)
    count_pair = pooled_pair[:, width : width + 1].astype(full)
    middle_pair = [middle_low, middle_x, middle_y, pairs["mid"]]
    rows_pair = [rows, pairs["x"], pairs["y"]]
    middles = middle_pair + [swap(p, "tensor", 1) for p in middle_pair]
    rows_core = [swap(p, "tensor", 1) for p in rows_pair]

    pos_logit = jnp.sum(pooled_pair[:, :width].astype(full) * positive, axis=1, keepdims=True) * inv_temp
    top_final = jnp.maximum(top, pos_logit)
    lse = top_final + jnp.log(total * jnp.exp(top - top_final) + jnp.exp(pos_logit - top_final))
    loss_part = jnp.broadcast_to((lse - pos_logit) / devices, (2, width))
    step = loss_scale * inv_temp
    pooled_grad = key_sum * (step * jnp.exp(top - lse)) + step * (jnp.exp(pos_logit - lse) - 1.0) * positive
    result_row = pooled_grad / count_pair
    vector_pair = result_row * final_gain
    vector_pair, rows_core = tie((vector_pair, rows_core))
    attn_grad, one_grad, sums = with_weights(
        ffn_back_kernel,
        "ffn_back",
        place,
        wholes,
        quarters,
        [slopes, summed, vector_pair, rows, affine],
        [S((length, width), low), S((length, width), full), S((8, width), full)],
    )
    vectors_far, vectors_core, rows_far, attn_grad, middles, sums, pooled_grad, loss_part, result_row = tie(
        (
            swap(vector_pair, "tensor", 2),
            swap(vector_pair, "tensor", 1),
            swap(pairs["x"], "tensor", 2),
            attn_grad,
            middles,
            sums,
            pooled_grad,
            loss_part,
            result_row,
        )
    )
    final_gain_part = result_row[0:1] * live_sum
    vectors_all = [vector_pair, vectors_far, vectors_core, swap(vectors_far, "tensor", 1)]
    rows_all = rows_pair + [rows_far] + rows_core + [swap(rows_far, "tensor", 1)]
    vectors = jnp.concatenate([final_gain_part, pooled_grad[0:1], sums[0:4], loss_part[0:1]])
    down, up, up_bias_half = ffn_weights(middles, rows_all, vectors_all, up_half, bias_half, down_half)
    vectors = vectors + swap(vectors, "tensor", 1)
    attn_far, attn_core, down, up, vectors = tie((swap(attn_grad, "tensor", 2), swap(attn_grad, "tensor", 1), down, up, vectors))
    attn_grads = [attn_grad, attn_far, attn_core, swap(attn_far, "tensor", 1)]

    near_in, away_in, qk_kept, qk_sent, vo_kept, vo_sent, query_bias_part, value_bias_part = attend_back(
        place, attn_grads, compact, query, keys, values, probs, context, query_weight.T, key_weight.T, value_weight.T, out_weight
    )
    line = lax.axis_size("dp") == 4
    moved = inward(down) if line else down
    qk_sent, vo_sent, near_in, away_in, moved, vectors = tie((qk_sent, vo_sent, near_in, away_in, moved, vectors))
    vectors = vectors + swap(vectors, "tensor", 2)
    pad = jnp.zeros((1, width - 2 * mine), full)
    narrow = jnp.concatenate([query_bias_part, value_bias_part, pad], axis=1)
    blank = jnp.zeros_like(up_bias_half)
    up_bias_part = jnp.concatenate([jnp.where(f == 0, up_bias_half, blank), jnp.where(f == 0, blank, up_bias_half)], axis=1)
    vectors = jnp.concatenate([vectors, narrow, up_bias_part, jnp.zeros((7, width), full)])
    extra = carried(vectors)
    if line:
        up_in = inward(up)
        qk = plus(qk_kept, swap(qk_sent, "fsdp", 1))
        vo = plus_carried(jnp.concatenate([vo_kept, extra]), swap(jnp.concatenate([vo_sent, extra]), "fsdp", 1), mine)
        down = plus(down, moved)
        down = plus(down, across(down))
        qk, up_in = tie((qk, up_in))
        up = plus(up, up_in)
        vo, down = tie((vo, down))
        qk = plus(qk, inward(qk))
        vo = plus_carried(vo, inward(vo), mine)
        up = plus(up, across(up))
        up, vo = tie((up, vo))
        qk = plus(qk, across(qk))
        down = outward(down)
        vo = plus_carried(vo, across(vo), mine)
        up = outward(up)
        qk = outward(qk)
        vo = outward(vo)
        extra, vo = vo[mine:].astype(full), vo[:mine]
        vectors = extra[:16] + extra[16:]
    else:
        down, up, qk, vo = [
            lax.psum(a.astype(full), "dp").astype(low)
            for a in (down, up, plus(qk_kept, swap(qk_sent, "fsdp", 1)), plus(vo_kept, swap(vo_sent, "fsdp", 1)))
        ]
        vectors = lax.psum(vectors + swap(vectors, "fsdp", 1), "dp")
    down_other, up_other, qk_other, vo_other = [swap(a, "fsdp", 1) for a in (down, up, qk, vo)]
    down_weight_grad = jnp.concatenate(ordered(down, down_other, f)).astype(full)
    up_weight_grad = jnp.concatenate(ordered(up, up_other, f), axis=1).astype(full)
    query_grad, key_grad = ordered(qk, qk_other, f)
    value_grad, out_grad = ordered(vo, vo_other, f)

    other_in = swap(away_in, "tensor", 1)
    far_in = swap(plus(near_in[1], other_in[1]), "tensor", 2)
    back = near_in[0].astype(full) + other_in[0].astype(full) + far_in.astype(full)
    compact_grad = (one_grad + back).astype(low)
    input_grad = dot(table, compact_grad, ((0,), (0,))).astype(low)
    return (
        output,
        input_grad[None],
        query_grad.T.astype(full),
        vectors[7, :mine],
        key_grad.T.astype(full),
        value_grad.T.astype(full),
        vectors[7, mine : 2 * mine],
        out_grad.astype(full),
        vectors[5],
        vectors[2],
        vectors[3],
        up_weight_grad,
        vectors[8],
        down_weight_grad,
        vectors[4],
        vectors[0],
        vectors[1],
        vectors[6, 0],
    )


def solution(mesh):
    placed = (
        P(("dp", "fsdp"), None, None),
        P(("dp", "fsdp"), None),
        P(("dp", "fsdp")),
        P(),
        P(("dp", "fsdp"), None),
        P(("dp", "fsdp"), None),
        P(None, "tensor"),
        P("tensor"),
        P(None, "tensor"),
        P(None, "tensor"),
        P("tensor"),
        P("tensor", None),
        P(),
        P(),
        P(),
        P(None, "tensor"),
        P("tensor"),
        P("tensor", None),
        P(),
        P(),
        P(),
    )
    return jax.shard_map(
        per_device,
        mesh=mesh,
        in_specs=placed,
        out_specs=(
            P(("dp", "fsdp", "tensor"), None, None),
            P(("dp", "fsdp", "tensor"), None, None),
            P(None, "tensor"),
            P("tensor"),
            P(None, "tensor"),
            P(None, "tensor"),
            P("tensor"),
            P("tensor", None),
            P(),
            P(),
            P(),
            P(None, "tensor"),
            P("tensor"),
            P("tensor", None),
            P(),
            P(),
            P(),
            P(),
        ),
        check_vma=False,
    )
```
